32 devices in a mesh: wide: 8 (over y, x, core), blk: 4 (over z).
Axes of the slice: x: 2, y: 2, z: 4, core: 2. Of those that a mesh axis runs over, the one named last changes fastest.
Arguments:
- left_points: float32 [4096], P(('wide', 'blk')), may hold values from -1 to 1, as said below
- left_ports: int32 [4096], P(('wide', 'blk')), may hold values from 0 to 63
- left_values: bfloat16 [4096, 64], P(('wide', 'blk')), may hold values from -6 to 6
- right_points: float32 [2048], P('blk'), may hold values from -1 to 1
- right_ports: int32 [2048], P('blk'), may hold values from 0 to 63
- right_values: bfloat16 [2048, 64], P('blk'), may hold values from -6 to 6
- sketch_block: int32 [2048], P('blk'), may hold values from 0 to 63, as said below
- sketch_weight: bfloat16 [2048], P('blk'), may hold values from -1 to 1
Outputs:
- basis: float32 [4096, 64], P(('wide', 'blk'))
- projected: float32 [64, 64], replicated
The draws below stay inside these ranges and needn't reach their ends.
Inputs may be any that keep to these rules, and one draw needn't show every extreme that they name: `left_points`: no left point lies closer than 0.6 / 2048 to any right point. `sketch_block`: in every aligned run of 64 right samples each sketch column appears exactly once.
All inputs are finite; a program needn't handle non-finite values.
Results may differ from the reference program's by a relative error of at most 0.0019.
Values sent between devices are 32-bit elements; how exact they have to be, the bound alone decides.
No kernel may reach another device: no remote copies, remote signals or barrier semaphores. Data moves between devices by JAX's collectives and lax.ppermute only.
A program may use at most 64 MiB of HBM per device.

```python
import jax
import jax.numpy as jnp
from jax import lax

PORTS = 64
K = 64
NL = 4096
NR = 2048


def draw_left_points(key, part):
    key_cell = jax.random.fold_in(key, 11)
    key_offset = jax.random.fold_in(key, 12)
    cell_index = jax.random.randint(key_cell, (NL,), 0, NR)
    jitter = jax.random.uniform(key_offset, (NL,), jnp.float32)
    spacing = 2.0 / NR
    return (-1.0 + (cell_index.astype(jnp.float32) + 0.5 + 0.2 * jitter) * spacing).astype(jnp.float32)


def draw_right_points(key, part):
    key_cell = jax.random.fold_in(key, 21)
    key_offset = jax.random.fold_in(key, 22)
    cell_index = jax.random.randint(key_cell, (NR,), 0, NR)
    jitter = jax.random.uniform(key_offset, (NR,), jnp.float32)
    spacing = 2.0 / NR
    return (-1.0 + (cell_index.astype(jnp.float32) + 0.2 * jitter) * spacing).astype(jnp.float32)


def draw_sketch_block(key, part):
    group_count = NR // K
    group_keys = jax.random.split(jax.random.fold_in(key, 31), group_count)
    orders = jax.vmap(lambda single: jax.random.permutation(single, K))(group_keys)
    return orders.reshape(NR).astype(jnp.int32)


def touch_ends(entries, rng, smallest, largest):
    longest = entries.shape.index(max(entries.shape))
    spots = []
    for shift in (0, 1):
        where = [jax.random.randint(jax.random.fold_in(rng, axis), (), 0, length) for axis, length in enumerate(entries.shape)]
        where[longest] = (where[longest] + shift) % entries.shape[longest]
        spots.append(tuple(where))
    return entries.at[spots[0]].set(smallest).at[spots[1]].set(largest)


def level_of(key, shape, pieces, low, high):
    def one(axis_at, shards_of):
        heights = jax.random.uniform(jax.random.fold_in(jax.random.fold_in(key, 6), axis_at), (shards_of,), jnp.float32, low / len(pieces), high / len(pieces))
        return jnp.repeat(jnp.exp(heights), shape[axis_at] // shards_of).reshape((-1,) + (1,) * (len(shape) - axis_at - 1))

    level = one(*pieces[0])
    for cut in pieces[1:]:
        level = level * one(*cut)
    return level


def normal_values(stream_key, extent, width, bound, cuts=(), kind=jnp.bfloat16):
    entries = jax.random.normal(stream_key, extent, jnp.float32) * width
    if len(cuts) > 0:
        entries = level_of(stream_key, extent, cuts, -0.22, 0.18) * entries
    return jnp.clip(entries, min=-bound, max=bound).astype(kind)


def setup_inputs(seed: int = 0) -> dict:
    splits = jax.random.split(jax.random.key(seed), 9)
    left_points = draw_left_points(jax.random.fold_in(splits[8], 71), 0)
    left_ports = touch_ends(jax.random.randint(splits[1], (NL,), 0, PORTS), jax.random.fold_in(splits[1], 1), 0, PORTS - 1).astype(jnp.int32)
    left_values = normal_values(splits[2], (NL, PORTS), 1.0, 6.0, ((0, 32),))
    right_points = draw_right_points(jax.random.fold_in(splits[8], 71), 0)
    right_ports = touch_ends(jax.random.randint(splits[4], (NR,), 0, PORTS), jax.random.fold_in(splits[4], 1), 0, PORTS - 1).astype(jnp.int32)
    right_values = normal_values(splits[5], (NR, PORTS), 1.0, 6.0, ((0, 4),))
    sketch_block = draw_sketch_block(jax.random.fold_in(splits[8], 71), 0)
    sketch_weight = normal_values(splits[7], (NR,), (NR // K) ** -0.5, 1.0, ((0, 4),))
    return dict(left_points=left_points, left_ports=left_ports, left_values=left_values, right_points=right_points, right_ports=right_ports, right_values=right_values, sketch_block=sketch_block, sketch_weight=sketch_weight)


def cholesky_lower(gram):
    order = gram.shape[0]
    index_ids = jnp.arange(order, dtype=jnp.int32)

    def column_step(j, lower):
        row_j = lax.dynamic_slice_in_dim(lower, j, 1, 0)[0]
        column = lax.dynamic_slice_in_dim(gram, j, 1, 1)[:, 0] - jnp.dot(lower, row_j, precision=lax.Precision.HIGHEST)
        pivot = jnp.sqrt(lax.dynamic_slice_in_dim(column, j, 1, 0)[0])
        fresh = jnp.where(index_ids > j, column / pivot, jnp.where(index_ids == j, pivot, jnp.zeros((), gram.dtype)))
        marker = (index_ids == j).astype(gram.dtype)
        return lower + fresh[:, None] * marker[None, :]
    return lax.fori_loop(0, order, column_step, jnp.zeros_like(gram))

def solve_lower(lower, rhs):
    order = lower.shape[0]
    index_ids = jnp.arange(order, dtype=jnp.int32)

    def row_step(j, result):
        row_j = lax.dynamic_slice_in_dim(lower, j, 1, 0)[0]
        pivot = lax.dynamic_slice_in_dim(row_j, j, 1, 0)[0]
        target = lax.dynamic_slice_in_dim(rhs, j, 1, 0)[0]
        value = (target - jnp.dot(row_j, result, precision=lax.Precision.HIGHEST)) / pivot
        marker = (index_ids == j).astype(rhs.dtype)
        return result + marker[:, None] * value[None, :]
    return lax.fori_loop(0, order, row_step, jnp.zeros_like(rhs))

def solve_upper(upper, rhs):
    order = upper.shape[0]
    index_ids = jnp.arange(order, dtype=jnp.int32)

    def row_step(step, result):
        j = order - 1 - step
        row_j = lax.dynamic_slice_in_dim(upper, j, 1, 0)[0]
        pivot = lax.dynamic_slice_in_dim(row_j, j, 1, 0)[0]
        target = lax.dynamic_slice_in_dim(rhs, j, 1, 0)[0]
        value = (target - jnp.dot(row_j, result, precision=lax.Precision.HIGHEST)) / pivot
        marker = (index_ids == j).astype(rhs.dtype)
        return result + marker[:, None] * value[None, :]
    return lax.fori_loop(0, order, row_step, jnp.zeros_like(rhs))

def reference(left_points, left_ports, left_values, right_points, right_ports, right_values, sketch_block, sketch_weight):
    left_freq = left_points.astype(jnp.float32)
    left_vals = left_values.astype(jnp.float32)
    total_right = right_points.shape[0]
    block_width = 256 if total_right % 256 == 0 else total_right
    block_count = total_right // block_width
    right_freq = right_points.astype(jnp.float32).reshape(block_count, block_width)
    ports_blocks = right_ports.reshape(block_count, block_width)
    values_blocks = right_values.astype(jnp.float32).reshape(block_count, block_width, PORTS)
    column_blocks = sketch_block.reshape(block_count, block_width)
    weight_blocks = sketch_weight.astype(jnp.float32).reshape(block_count, block_width)

    def absorb(carry, items):
        freq, ports, values_block, columns, weights = items
        num_v = left_vals[:, ports]
        num_w = values_block.T[left_ports]
        inverse = 1.0 / (left_freq[:, None] - freq[None, :])
        loewner = (num_v - num_w) * inverse
        shifted = (left_freq[:, None] * num_v - freq[None, :] * num_w) * inverse
        part_one = jax.ops.segment_sum((loewner * weights[None, :]).T, columns, num_segments=K)
        part_two = jax.ops.segment_sum((shifted * weights[None, :]).T, columns, num_segments=K)
        return ((carry[0] + part_one, carry[1] + part_two), None)
    start_carry = (jnp.zeros((K, left_points.shape[0]), jnp.float32), jnp.zeros((K, left_points.shape[0]), jnp.float32))
    (sketch_t, shifted_t), _ = lax.scan(absorb, start_carry, (right_freq, ports_blocks, values_blocks, column_blocks, weight_blocks))
    row_total = left_points.shape[0]
    gram = jnp.dot(sketch_t, sketch_t.T, precision=lax.Precision.HIGHEST) / row_total
    lower = cholesky_lower(gram)
    basis_t = solve_lower(lower, sketch_t)
    coefficient = jnp.dot(basis_t, shifted_t.T, precision=lax.Precision.HIGHEST) / row_total
    projected = solve_upper(lower.T, coefficient)
    return (basis_t.T, projected)
```

```python
import functools

import jax
import jax.numpy as jnp
from jax import lax
from jax.experimental import pallas as pl
from jax.experimental.pallas import tpu as pltpu
from jax.sharding import PartitionSpec as P

K = 64
LANES = 128
SUB = 8
HIGHEST = lax.Precision.HIGHEST


def swap(value, axis, distance):
    size = lax.axis_size(axis)
    return lax.ppermute(value, axis, [(i, i ^ distance) for i in range(size)])


def kernel_call(body, out_shape, **kw):
    return pl.pallas_call(body, out_shape=out_shape, **kw)


def pieces(value, count=3):
    out = []
    for _ in range(count - 1):
        top = value.astype(jnp.bfloat16)
        out.append(top)
        value = value - top.astype(jnp.float32)
    out.append(value.astype(jnp.bfloat16))
    return out


def dot(a, b, ca, cb, precision=None):
    return lax.dot_general(
        a, b, (((ca,), (cb,)), ((), ())), precision=precision, preferred_element_type=jnp.float32
    )


def pack_body(mu, lp, lv, lam, rp, rv, col, w, left, right):
    half = lv.shape[0] // 2
    left[:half, :K] = lv[:half, :].astype(jnp.float32)
    left[:half, K:] = lv[half:, :].astype(jnp.float32)
    left[half : half + 1, :] = mu[...]
    left[half + 1 : half + 2, :] = lp[...].astype(jnp.float32)
    left[half + 2 :, :] = jnp.zeros((left.shape[0] - half - 2, LANES), jnp.float32)
    half = rv.shape[0] // 2
    right[:half, :K] = rv[:half, :].astype(jnp.float32)
    right[:half, K:] = rv[half:, :].astype(jnp.float32)
    n = lam.shape[0]
    right[half : half + n, :] = lam[...]
    right[half + n : half + 2 * n, :] = rp[...].astype(jnp.float32)
    right[half + 2 * n : half + 3 * n, :] = col[...].astype(jnp.float32)
    right[half + 3 * n : half + 4 * n, :] = w[...]


def column(row):
    return jnp.broadcast_to(row, (LANES, LANES)).T


def sketch_body(n_left, n_right, *refs):
    lefts, rights, (pay, mu_out, hot_out) = refs[:n_left], refs[n_left : n_left + n_right], refs[n_left + n_right :]
    half = (lefts[0].shape[0] // SUB - 1) * SUB
    rows = LANES * n_left
    lane = lax.broadcasted_iota(jnp.int32, (LANES, LANES), 1).astype(jnp.float32)
    mus, hots, values = [], [], []
    for left in lefts:
        mus.append(column(left[half : half + 1, :]))
        ports = column(left[half + 1 : half + 2, :])
        hots.append(
            (
                jnp.where(ports == lane, 1.0, 0.0).astype(jnp.bfloat16),
                jnp.where(ports + K == lane, 1.0, 0.0).astype(jnp.bfloat16),
            )
        )
        values += [left[:half, :K].astype(jnp.bfloat16), left[:half, K:].astype(jnp.bfloat16)]
    values = jnp.concatenate(values, axis=0)
    low, high = jnp.concatenate([h[0] for h in hots], axis=0), jnp.concatenate([h[1] for h in hots], axis=0)
    total = jnp.zeros((rows, K), jnp.float32)
    cross = jnp.zeros((K, LANES), jnp.float32)
    first = lax.broadcasted_iota(jnp.int32, (K, LANES), 1) < K
    for right in rights:
        n = right.shape[0] * 2 // (LANES + SUB)
        depth = n * K
        table = right[:depth, :].astype(jnp.bfloat16)
        seconds = []
        for part in range(2):
            spots = range(part * n // 2, (part + 1) * n // 2)

            def along(which):
                return jnp.concatenate(
                    [right[depth + which * n + s : depth + which * n + s + 1, :] for s in spots], axis=1
                )

            width = LANES * len(spots)
            index = lax.broadcasted_iota(jnp.int32, (K, width), 0).astype(jnp.float32)
            lam = along(0)
            pick = jnp.where(along(1) == index, 1.0, 0.0).astype(jnp.bfloat16)
            omega = jnp.where(along(2) == index, along(3), 0.0).astype(jnp.bfloat16)
            upper = dot(values, pick, 1, 0)
            lower = dot(high if part else low, table, 1, 1)
            scale = jnp.concatenate(
                [jnp.concatenate([m] * len(spots), axis=1) for m in mus], axis=0
            ) - lam
            loewner = (upper - lower) / scale
            for piece in pieces(loewner):
                total = total + dot(piece, omega, 1, 1)
            seconds.append(dot(omega, table, 1, 0))
        cross = cross + jnp.where(first, seconds[0], seconds[1])
    cross = cross[:, :K] + cross[:, K:]
    pay[: rows // 2, :] = jnp.concatenate([total[: rows // 2], total[rows // 2 :]], axis=1)
    pay[rows // 2 :, :] = jnp.concatenate([cross[: K // 2], cross[K // 2 :]], axis=1)
    mus = jnp.concatenate(mus, axis=0)
    ohs = low[:, :K].astype(jnp.float32)
    mu_out[...] = jnp.concatenate([mus[: rows // 2, :K], mus[rows // 2 :, K:]], axis=1)
    hot_out[...] = jnp.concatenate([ohs[: rows // 2], ohs[rows // 2 :]], axis=1)


def moments_body(own, other, mu, hot, gc, full):
    depth = mu.shape[0]
    sketch = own[:depth, :] + other[:depth, :]
    cross = own[depth:, :] + other[depth:, :]
    cross = jnp.concatenate([cross[:, :K], cross[:, K:]], axis=0)
    zero = jnp.zeros_like(cross)
    wide = jnp.concatenate(
        [jnp.concatenate([cross, zero], axis=1), jnp.concatenate([zero, cross], axis=1)], axis=0
    )
    shifted = mu[...] * sketch
    ohs = hot[...].astype(jnp.bfloat16)
    for piece in pieces(wide):
        shifted = shifted + dot(ohs, piece, 1, 1)
    both = dot(sketch, jnp.concatenate([sketch, shifted], axis=1), 0, 0, HIGHEST)
    gc[...] = jnp.concatenate(
        [both[:K, :K] + both[K:, K:LANES], both[:K, LANES : LANES + K] + both[K:, LANES + K :]], axis=1
    )
    full[...] = sketch


def finish_body(scale, place, own, other, sketch, basis, projected):
    gc = (own[...] + other[...]) * scale
    lane = lax.broadcasted_iota(jnp.int32, (SUB, LANES), 1)
    sub = lax.broadcasted_iota(jnp.int32, (SUB, LANES), 0)
    blocks = []
    for r in range(K // SUB):
        blocks.append(
            jnp.where(lane < K, gc[r * SUB : (r + 1) * SUB, :], jnp.where(lane == sub + (K + r * SUB), 1.0, 0.0))
        )
    for j in range(K):
        r, s = divmod(j, SUB)
        row = blocks[r][s : s + 1, :]
        row = row / row[:, j : j + 1]
        for q in range(r, K // SUB):
            factor = blocks[q][:, j : j + 1]
            if q == r:
                if s == SUB - 1:
                    continue
                factor = jnp.where(sub[:, :1] > s, factor, 0.0)
            blocks[q] = blocks[q] - factor * row
    done = []
    for r in range(K // SUB):
        pivot = jnp.sum(jnp.where(lane == sub + r * SUB, blocks[r], 0.0), axis=1, keepdims=True)
        done.append(blocks[r][:, K:] / jnp.sqrt(pivot))
    inverse = jnp.concatenate(done, axis=0)
    rows = basis.shape[0]
    spots = sketch.shape[0] // rows
    mine = place[0]
    start = pl.multiple_of(lax.rem(mine, spots) * rows, rows)
    picked = sketch[pl.ds(start, rows), :]
    picked = jnp.where(mine < spots, picked[:, :K], picked[:, K:])
    basis[...] = dot(picked, inverse, 1, 1, HIGHEST)
    coefficient = dot(inverse, gc[:, K:], 1, 0, HIGHEST)
    projected[...] = dot(inverse, coefficient, 0, 0, HIGHEST)


def per_device(left_points, left_ports, left_values, right_points, right_ports, right_values, sketch_block, sketch_weight):
    f32 = jnp.float32
    rows, rights = left_points.shape[0], right_points.shape[0]
    blk, wide = lax.axis_size("blk"), lax.axis_size("wide")
    along = (rights // LANES, LANES)
    left, right = kernel_call(
        pack_body,
        (
            jax.ShapeDtypeStruct((rows // 2 + SUB, LANES), f32),
            jax.ShapeDtypeStruct((rights // 2 + 4 * along[0], LANES), f32),
        ),
    )(
        left_points.reshape(1, rows),
        left_ports.reshape(1, rows),
        left_values,
        right_points.reshape(along),
        right_ports.reshape(along),
        right_values,
        sketch_block.reshape(along),
        sketch_weight.astype(f32).reshape(along),
    )
    rights_held = [right, swap(right, "blk", 1)]
    place = lax.axis_index("blk")
    lefts, steps = [left], []
    distance = 2
    while distance < blk:
        got = [swap(v, "blk", distance) for v in lefts]
        here = (place // distance) % 2 == 0
        lefts = [jnp.where(here, a, b) for a, b in zip(lefts, got)] + [jnp.where(here, b, a) for a, b in zip(lefts, got)]
        steps.append(distance)
        distance *= 2
    held = rows * len(lefts)
    pay, mu, hot = kernel_call(
        functools.partial(sketch_body, len(lefts), len(rights_held)),
        (
            jax.ShapeDtypeStruct((held // 2 + K // 2, LANES), f32),
            jax.ShapeDtypeStruct((held // 2, LANES), f32),
            jax.ShapeDtypeStruct((held // 2, LANES), f32),
        ),
    )(*lefts, *rights_held)
    for distance in steps[:-1]:
        pay = pay + swap(pay, "blk", distance)
    gc, sketch = kernel_call(
        moments_body,
        (jax.ShapeDtypeStruct((K, LANES), f32), jax.ShapeDtypeStruct((held // 2, LANES), f32)),
    )(pay, swap(pay, "blk", steps[-1]), mu, hot)
    hops = [("blk", 1)]
    distance = 2
    while distance < wide:
        hops.append(("wide", distance))
        distance *= 2
    for axis, distance in hops:
        gc = gc + swap(gc, axis, distance)
    basis, projected = kernel_call(
        functools.partial(finish_body, 1.0 / (rows * blk * wide)),
        (jax.ShapeDtypeStruct((rows, K), f32), jax.ShapeDtypeStruct((K, K), f32)),
        in_specs=[pl.BlockSpec(memory_space=pltpu.SMEM)] + [pl.BlockSpec(memory_space=pltpu.VMEM)] * 3,
    )(jnp.reshape(place // 2, (1,)), gc, swap(gc, "wide", 1), sketch)
    return basis, projected


def solution(mesh):
    split = P(("wide", "blk"))
    return jax.shard_map(
        per_device,
        mesh=mesh,
        in_specs=(split, split, P(("wide", "blk"), None), P("blk"), P("blk"), P("blk", None), P("blk"), P("blk")),
        out_specs=(P(("wide", "blk"), None), P()),
        check_vma=False,
    )
```

```python
import functools

import jax
import jax.numpy as jnp
from jax import lax
from jax.experimental import pallas as pl
from jax.experimental.pallas import tpu as pltpu
from jax.sharding import PartitionSpec as P

K = 64
LANES = 128
SUB = 8
HIGHEST = lax.Precision.HIGHEST
VMEM_LIMIT = 8 << 20


def swap(value, axis, distance):
    size = lax.axis_size(axis)
    return lax.ppermute(value, axis, [(i, i ^ distance) for i in range(size)])


def kernel_call(body, out_shape, operands, limit=VMEM_LIMIT, **kw):
    return pl.pallas_call(
        body, out_shape=out_shape, compiler_params=pltpu.CompilerParams(vmem_limit_bytes=limit), **kw
    )(*operands)


def pieces(value, count=3):
    out = []
    for _ in range(count - 1):
        top = value.astype(jnp.bfloat16)
        out.append(top)
        value = value - top.astype(jnp.float32)
    out.append(value.astype(jnp.bfloat16))
    return out


def dot(a, b, ca, cb, precision=None):
    return lax.dot_general(
        a, b, (((ca,), (cb,)), ((), ())), precision=precision, preferred_element_type=jnp.float32
    )


def pack_body(mu, lp, lv, lam, rp, rv, col, w, left, right):
    left[:K, :] = lv[...].astype(jnp.float32)
    left[K : K + 1, :] = mu[...]
    left[K + 1 : K + 2, :] = lp[...].astype(jnp.float32)
    left[K + 2 :, :] = jnp.zeros((left.shape[0] - K - 2, LANES), jnp.float32)
    right[:K, :] = rv[...].astype(jnp.float32)
    weights = w[...].astype(jnp.float32)
    for s in range(lam.shape[0]):
        lanes = pl.ds(s * LANES, LANES)
        right[K : K + 1, lanes] = lam[s : s + 1, :]
        right[K + 1 : K + 2, lanes] = rp[s : s + 1, :].astype(jnp.float32)
        right[K + 2 : K + 3, lanes] = col[s : s + 1, :].astype(jnp.float32)
        right[K + 3 : K + 4, lanes] = weights[s : s + 1, :]
    right[K + 4 :, :] = jnp.zeros((right.shape[0] - K - 4, right.shape[1]), jnp.float32)


def in_order(lefts, distance):
    half = len(lefts) // 2
    here = lax.rem(lax.div(lax.axis_index("blk"), distance), 2) == 0
    own, got = [ref[...] for ref in lefts[:half]], [ref[...] for ref in lefts[half:]]
    return [jnp.where(here, a, b) for a, b in zip(own, got)] + [jnp.where(here, b, a) for a, b in zip(own, got)]


def sketch_body(n_left, distance, *refs):
    lefts, rights, (pay, freq, ports) = in_order(refs[:n_left], distance), refs[n_left:-3], refs[-3:]
    index = lax.broadcasted_iota(jnp.int32, (K, LANES), 0).astype(jnp.float32)
    mus, sides = [], []
    for q, left in enumerate(lefts):
        mu, port = left[K : K + 1, :], left[K + 1 : K + 2, :]
        freq[q : q + 1, :] = mu
        ports[q : q + 1, :] = port
        mus.append(jnp.broadcast_to(mu, (LANES, LANES)).T)
        sides.append(jnp.concatenate([left[:K, :], jnp.where(port == index, -1.0, 0.0)], axis=0).T.astype(jnp.bfloat16))
    side = jnp.concatenate(sides, axis=0)
    rows = side.shape[0]
    total = jnp.zeros((rows, K), jnp.float32)
    cross = jnp.zeros((K, K), jnp.float32)
    for right in rights:
        width = right.shape[1]
        index = lax.broadcasted_iota(jnp.int32, (K, width), 0).astype(jnp.float32)
        values = right[:K, :].astype(jnp.bfloat16)
        lam = right[K : K + 1, :]
        pick = jnp.where(right[K + 1 : K + 2, :] == index, 1.0, 0.0).astype(jnp.bfloat16)
        omega = jnp.where(right[K + 2 : K + 3, :] == index, right[K + 3 : K + 4, :], 0.0).astype(jnp.bfloat16)
        upper = dot(side, jnp.concatenate([pick, values], axis=0), 1, 0)
        scale = jnp.concatenate([jnp.concatenate([m] * (width // LANES), axis=1) for m in mus], axis=0) - lam
        loewner = upper / scale
        for piece in pieces(loewner):
            total = total + dot(piece, omega, 1, 1)
        cross = cross + dot(omega, values, 1, 1)
    for q in range(n_left):
        pay[q * K : (q + 1) * K, :] = total[q * LANES : (q + 1) * LANES, :].T
    pay[n_left * K :, :] = jnp.concatenate([cross[: K // 2], cross[K // 2 :]], axis=1)


def moments_body(own, other, freq, ports, gc, full):
    n_left = freq.shape[0]
    both = own[...] + other[...]
    index = lax.broadcasted_iota(jnp.int32, (K, LANES), 0).astype(jnp.float32)
    cross = both[n_left * K :, :]
    cross = pieces(jnp.concatenate([cross[:, :K], cross[:, K:]], axis=0))
    sketches, shifts = [], []
    for q in range(n_left):
        sketch = both[q * K : (q + 1) * K, :]
        hot = jnp.where(ports[q : q + 1, :] == index, 1.0, 0.0).astype(jnp.bfloat16)
        shift = freq[q : q + 1, :] * sketch
        for piece in cross:
            shift = shift + dot(piece, hot, 1, 0)
        sketches.append(sketch)
        shifts.append(shift)
    sketch = jnp.concatenate(sketches, axis=1)
    gc[...] = dot(sketch, jnp.concatenate([sketch, jnp.concatenate(shifts, axis=1)], axis=0), 1, 1, HIGHEST)
    full[...] = both[: n_left * K, :]


def finish_body(scale, own, other, sketch, basis, projected):
    gc = (own[...] + other[...]) * scale
    lane = lax.broadcasted_iota(jnp.int32, (SUB, LANES), 1)
    sub = lax.broadcasted_iota(jnp.int32, (SUB, LANES), 0)
    blocks = []
    for r in range(K // SUB):
        blocks.append(
            jnp.where(lane < K, gc[r * SUB : (r + 1) * SUB, :], jnp.where(lane == sub + (K + r * SUB), 1.0, 0.0))
        )
    for j in range(K):
        r, s = divmod(j, SUB)
        row = blocks[r][s : s + 1, :]
        row = row / row[:, j : j + 1]
        for q in range(r, K // SUB):
            factor = blocks[q][:, j : j + 1]
            if q == r:
                if s == SUB - 1:
                    continue
                factor = jnp.where(sub[:, :1] > s, factor, 0.0)
            blocks[q] = blocks[q] - factor * row
    done = []
    for r in range(K // SUB):
        pivot = jnp.sum(jnp.where(lane == sub + r * SUB, blocks[r], 0.0), axis=1, keepdims=True)
        done.append(blocks[r][:, K:] / jnp.sqrt(pivot))
    inverse = jnp.concatenate(done, axis=0)
    mine = pl.multiple_of(lax.div(lax.axis_index("blk"), 2) * K, K)
    basis[...] = dot(inverse, sketch[pl.ds(mine, K), :], 1, 0, HIGHEST)
    coefficient = dot(inverse, gc[:, K:], 1, 0, HIGHEST)
    projected[...] = dot(inverse, coefficient, 0, 0, HIGHEST)


def per_device(left_points, left_ports, left_values, right_points, right_ports, right_values, sketch_block, sketch_weight):
    f32 = jnp.float32
    rows, rights = left_points.shape[0], right_points.shape[0]
    blk, wide = lax.axis_size("blk"), lax.axis_size("wide")
    along = (rights // LANES, LANES)
    left, right = kernel_call(
        pack_body,
        (jax.ShapeDtypeStruct((K + SUB, LANES), f32), jax.ShapeDtypeStruct((K + SUB, rights), f32)),
        (
            left_points.reshape(1, rows),
            left_ports.reshape(1, rows),
            left_values.T,
            right_points.reshape(along),
            right_ports.reshape(along),
            right_values.T,
            sketch_block.reshape(along),
            sketch_weight.reshape(along),
        ),
    )
    place = lax.axis_index("blk")
    lefts, distance = [left], 2
    while True:
        got = [swap(v, "blk", distance) for v in lefts]
        if distance * 2 >= blk:
            break
        here = (place // distance) % 2 == 0
        lefts = [jnp.where(here, a, b) for a, b in zip(lefts, got)] + [jnp.where(here, b, a) for a, b in zip(lefts, got)]
        distance *= 2
    lefts = lefts + got
    rights_held = [right, swap(right, "blk", 1)]
    held = len(lefts)
    pay, freq, ports = kernel_call(
        functools.partial(sketch_body, held, distance),
        (
            jax.ShapeDtypeStruct((held * K + K // 2, LANES), f32),
            jax.ShapeDtypeStruct((held, LANES), f32),
            jax.ShapeDtypeStruct((held, LANES), f32),
        ),
        (*lefts, *rights_held),
        limit=max(VMEM_LIMIT, held * VMEM_LIMIT // 2),
    )
    step = 2
    while step < distance:
        pay = pay + swap(pay, "blk", step)
        step *= 2
    gc, sketch = kernel_call(
        moments_body,
        (jax.ShapeDtypeStruct((K, LANES), f32), jax.ShapeDtypeStruct((held * K, LANES), f32)),
        (pay, swap(pay, "blk", distance), freq, ports),
    )
    hops = [("blk", 1)]
    distance = 2
    while distance < wide:
        hops.append(("wide", distance))
        distance *= 2
    for axis, distance in hops:
        gc = gc + swap(gc, axis, distance)
    basis, projected = kernel_call(
        functools.partial(finish_body, 1.0 / (rows * blk * wide)),
        (jax.ShapeDtypeStruct((K, rows), f32), jax.ShapeDtypeStruct((K, K), f32)),
        (gc, swap(gc, "wide", 1), sketch),
    )
    return basis.T, projected


def solution(mesh):
    split = P(("wide", "blk"))
    return jax.shard_map(
        per_device,
        mesh=mesh,
        in_specs=(split, split, P(("wide", "blk"), None), P("blk"), P("blk"), P("blk", None), P("blk"), P("blk")),
        out_specs=(P(("wide", "blk"), None), P()),
        check_vma=False,
    )
```

```python
import functools

import jax
import jax.numpy as jnp
from jax import lax
from jax.experimental import pallas as pl
from jax.experimental.pallas import tpu as pltpu
from jax.sharding import PartitionSpec as P

K = 64
LANES = 128
SUB = 8
HIGHEST = lax.Precision.HIGHEST
VMEM_LIMIT = 8 << 20


def swap(value, blk=0, wide=0):
    wides, blks = lax.axis_size("wide"), lax.axis_size("blk")
    pairs = [(w * blks + b, (w ^ wide) * blks + (b ^ blk)) for w in range(wides) for b in range(blks)]
    return lax.ppermute(value, ("wide", "blk"), pairs)


def kernel_call(body, out_shape, operands, limit=VMEM_LIMIT, **kw):
    return pl.pallas_call(
        body, out_shape=out_shape, compiler_params=pltpu.CompilerParams(vmem_limit_bytes=limit), **kw
    )(*operands)


def pieces(value, count=3):
    out = []
    for _ in range(count - 1):
        top = value.astype(jnp.bfloat16)
        out.append(top)
        value = value - top.astype(jnp.float32)
    out.append(value.astype(jnp.bfloat16))
    return out


def dot(a, b, ca, cb, precision=None):
    return lax.dot_general(
        a, b, (((ca,), (cb,)), ((), ())), precision=precision, preferred_element_type=jnp.float32
    )


def pack_body(*refs):
    sources, (left, right), held, sems = refs[:8], refs[8:10], refs[10:18], refs[18]
    copies = [pltpu.make_async_copy(a, b, sems.at[i]) for i, (a, b) in enumerate(zip(sources, held))]
    for copy in copies:
        copy.start()
    mu, lp, lv, lam, rp, rv, col, w = held
    left[K + 2 :, :] = jnp.zeros((left.shape[0] - K - 2, LANES), jnp.float32)
    right[K + 4 :, :] = jnp.zeros((right.shape[0] - K - 4, right.shape[1]), jnp.float32)
    for copy in copies:
        copy.wait()
    left[:K, :] = lv[...].astype(jnp.float32)
    left[K : K + 1, :] = mu[...]
    left[K + 1 : K + 2, :] = lp[...].astype(jnp.float32)
    right[:K, :] = rv[...].astype(jnp.float32)
    weights = w[...].astype(jnp.float32)
    for s in range(lam.shape[0]):
        lanes = pl.ds(s * LANES, LANES)
        right[K : K + 1, lanes] = lam[s : s + 1, :]
        right[K + 1 : K + 2, lanes] = rp[s : s + 1, :].astype(jnp.float32)
        right[K + 2 : K + 3, lanes] = col[s : s + 1, :].astype(jnp.float32)
        right[K + 3 : K + 4, lanes] = weights[s : s + 1, :]


def in_order(lefts, distance):
    half = len(lefts) // 2
    here = lax.rem(lax.div(lax.axis_index("blk"), distance), 2) == 0
    own, got = [ref[...] for ref in lefts[:half]], [ref[...] for ref in lefts[half:]]
    return [jnp.where(here, a, b) for a, b in zip(own, got)] + [jnp.where(here, b, a) for a, b in zip(own, got)]


def sketch_body(n_left, distance, *refs):
    lefts, rights, (pay, freq, ports) = in_order(refs[:n_left], distance), refs[n_left:-3], refs[-3:]
    index = lax.broadcasted_iota(jnp.int32, (K, LANES), 0).astype(jnp.float32)
    mus, sides = [], []
    for q, left in enumerate(lefts):
        mu, port = left[K : K + 1, :], left[K + 1 : K + 2, :]
        freq[q : q + 1, :] = mu
        ports[q : q + 1, :] = port
        mus.append(jnp.broadcast_to(mu, (LANES, LANES)).T)
        sides.append(jnp.concatenate([left[:K, :], jnp.where(port == index, -1.0, 0.0)], axis=0).T.astype(jnp.bfloat16))
    side = jnp.concatenate(sides, axis=0)
    rows = side.shape[0]
    total = jnp.zeros((rows, K), jnp.float32)
    cross = jnp.zeros((K, K), jnp.float32)
    for right in rights:
        width = right.shape[1]
        index = lax.broadcasted_iota(jnp.int32, (K, width), 0).astype(jnp.float32)
        values = right[:K, :].astype(jnp.bfloat16)
        lam = right[K : K + 1, :]
        pick = jnp.where(right[K + 1 : K + 2, :] == index, 1.0, 0.0).astype(jnp.bfloat16)
        omega = jnp.where(right[K + 2 : K + 3, :] == index, right[K + 3 : K + 4, :], 0.0).astype(jnp.bfloat16)
        upper = dot(side, jnp.concatenate([pick, values], axis=0), 1, 0)
        scale = jnp.concatenate([jnp.concatenate([m] * (width // LANES), axis=1) for m in mus], axis=0) - lam
        loewner = upper / scale
        for piece in pieces(loewner):
            total = total + dot(piece, omega, 1, 1)
        cross = cross + dot(omega, values, 1, 1)
    for q in range(n_left):
        pay[q * K : (q + 1) * K, :] = total[q * LANES : (q + 1) * LANES, :].T
    pay[n_left * K :, :] = jnp.concatenate([cross[: K // 2], cross[K // 2 :]], axis=1)


def moments_body(own, other, freq, ports, gc, full):
    n_left = freq.shape[0]
    both = own[...] + other[...]
    index = lax.broadcasted_iota(jnp.int32, (K, LANES), 0).astype(jnp.float32)
    cross = both[n_left * K :, :]
    cross = pieces(jnp.concatenate([cross[:, :K], cross[:, K:]], axis=0))
    sketches, shifts = [], []
    for q in range(n_left):
        sketch = both[q * K : (q + 1) * K, :]
        hot = jnp.where(ports[q : q + 1, :] == index, 1.0, 0.0).astype(jnp.bfloat16)
        shift = freq[q : q + 1, :] * sketch
        for piece in cross:
            shift = shift + dot(piece, hot, 1, 0)
        sketches.append(sketch)
        shifts.append(shift)
    sketch = jnp.concatenate(sketches, axis=1)
    gc[...] = dot(sketch, jnp.concatenate([sketch, jnp.concatenate(shifts, axis=1)], axis=0), 1, 1, HIGHEST)
    full[...] = both[: n_left * K, :]


def full(value):
    return jnp.broadcast_to(value, (SUB, LANES))


def inverse_factor(gram):
    lane = lax.broadcasted_iota(jnp.int32, (SUB, LANES), 1)
    sub = lax.broadcasted_iota(jnp.int32, (SUB, LANES), 0)
    count = K // SUB
    blocks = [
        jnp.where(lane < K, gram[r * SUB : (r + 1) * SUB, :], jnp.where(lane == sub + (K + r * SUB), 1.0, 0.0))
        for r in range(count)
    ]
    out = []
    for r in range(count):
        here, first = blocks[r], r * SUB
        below = range(r + 1, count)
        rows = [full(here[t : t + 1, :]) for t in range(SUB)]
        part = {(t, u): full(here[t : t + 1, first + u : first + u + 1]) for t in range(SUB) for u in range(t + 1)}
        cols = {q: [full(blocks[q][:, first + u : first + u + 1]) for u in range(SUB)] for q in below}
        inverse = []
        for u in range(SUB):
            inverse.append(1.0 / part[u, u])
            ratio = {t: part[t, u] * inverse[u] for t in range(u + 1, SUB)}
            for t in range(u + 1, SUB):
                for v in range(u + 1, t + 1):
                    part[t, v] = part[t, v] - (part[t, u] * part[v, u]) * inverse[u]
            for t in range(u + 1, SUB):
                rows[t] = rows[t] - ratio[t] * rows[u]
                for q in below:
                    cols[q][t] = cols[q][t] - ratio[t] * cols[q][u]
        done = jnp.zeros((SUB, LANES), jnp.float32)
        for t in range(SUB):
            done = jnp.where(sub == t, rows[t] * lax.rsqrt(part[t, t]), done)
        out.append(done[:, K:])
        rows = [row * inv for row, inv in zip(rows, inverse)]
        for q in below:
            terms = [col * row for col, row in zip(cols[q], rows)]
            while len(terms) > 1:
                terms = [a + b for a, b in zip(terms[::2], terms[1::2])]
            blocks[q] = blocks[q] - terms[0]
    return jnp.concatenate(out, axis=0)


def finish_body(scale, own, other, sketch, basis, projected):
    gc = (own[...] + other[...]) * scale
    inverse = inverse_factor(gc)
    mine = pl.multiple_of(lax.div(lax.axis_index("blk"), 2) * K, K)
    basis[...] = dot(inverse, sketch[pl.ds(mine, K), :], 1, 0, HIGHEST)
    coefficient = dot(inverse, gc[:, K:], 1, 0, HIGHEST)
    projected[...] = dot(inverse, coefficient, 0, 0, HIGHEST)


def per_device(left_points, left_ports, left_values, right_points, right_ports, right_values, sketch_block, sketch_weight):
    f32 = jnp.float32
    rows, rights = left_points.shape[0], right_points.shape[0]
    blk, wide = lax.axis_size("blk"), lax.axis_size("wide")
    along = (rights // LANES, LANES)
    left, right = kernel_call(
        pack_body,
        (jax.ShapeDtypeStruct((K + SUB, LANES), f32), jax.ShapeDtypeStruct((K + SUB, rights), f32)),
        tuple(pltpu.with_memory_space_constraint(v, pltpu.HBM) for v in (
            left_points.reshape(1, rows),
            left_ports.reshape(1, rows),
            left_values.T,
            right_points.reshape(along),
            right_ports.reshape(along),
            right_values.T,
            sketch_block.reshape(along),
            sketch_weight.reshape(along),
        )),
        in_specs=[pl.BlockSpec(memory_space=pltpu.HBM)] * 8,
        scratch_shapes=[
            pltpu.VMEM((1, rows), f32),
            pltpu.VMEM((1, rows), jnp.int32),
            pltpu.VMEM((K, rows), left_values.dtype),
            pltpu.VMEM(along, f32),
            pltpu.VMEM(along, jnp.int32),
            pltpu.VMEM((K, rights), right_values.dtype),
            pltpu.VMEM(along, jnp.int32),
            pltpu.VMEM(along, sketch_weight.dtype),
            pltpu.SemaphoreType.DMA((8,)),
        ],
    )
    place = lax.axis_index("blk")
    lefts, distance = [left], 2
    while True:
        got = [swap(v, distance) for v in lefts]
        if distance * 2 >= blk:
            break
        here = (place // distance) % 2 == 0
        lefts = [jnp.where(here, a, b) for a, b in zip(lefts, got)] + [jnp.where(here, b, a) for a, b in zip(lefts, got)]
        distance *= 2
    lefts = lefts + got
    rights_held = [right, swap(right, 1)]
    held = len(lefts)
    pay, freq, ports = kernel_call(
        functools.partial(sketch_body, held, distance),
        (
            jax.ShapeDtypeStruct((held * K + K // 2, LANES), f32),
            jax.ShapeDtypeStruct((held, LANES), f32),
            jax.ShapeDtypeStruct((held, LANES), f32),
        ),
        (*lefts, *rights_held),
        limit=max(VMEM_LIMIT, held * VMEM_LIMIT // 2),
    )
    step = 2
    while step < distance:
        pay = pay + swap(pay, step)
        step *= 2
    gc, sketch = kernel_call(
        moments_body,
        (jax.ShapeDtypeStruct((K, LANES), f32), jax.ShapeDtypeStruct((held * K, LANES), f32)),
        (pay, swap(pay, distance), freq, ports),
    )
    gc = gc + swap(gc, 0, 1)
    hops, distance = [(1, 1)], 2
    while distance < wide:
        hops.append((0, distance + 1))
        distance *= 2
    for hop in hops[:-1]:
        gc = gc + swap(gc, *hop)
    basis, projected = kernel_call(
        functools.partial(finish_body, 1.0 / (rows * blk * wide)),
        (jax.ShapeDtypeStruct((K, rows), f32), jax.ShapeDtypeStruct((K, K), f32)),
        (gc, swap(gc, *hops[-1]), sketch),
    )
    return basis.T, projected


def solution(mesh):
    split = P(("wide", "blk"))
    return jax.shard_map(
        per_device,
        mesh=mesh,
        in_specs=(split, split, P(("wide", "blk"), None), P("blk"), P("blk"), P("blk", None), P("blk"), P("blk")),
        out_specs=(P(("wide", "blk"), None), P()),
        check_vma=False,
    )
```

```python
import functools

import jax
import jax.numpy as jnp
from jax import lax
from jax.experimental import pallas as pl
from jax.experimental.pallas import tpu as pltpu
from jax.sharding import PartitionSpec as P

K = 64
LANES = 128
SUB = 8
HIGHEST = lax.Precision.HIGHEST
VMEM_LIMIT = 8 << 20


def swap(value, blk=0, wide=0):
    wides, blks = lax.axis_size("wide"), lax.axis_size("blk")
    pairs = [(w * blks + b, (w ^ wide) * blks + (b ^ blk)) for w in range(wides) for b in range(blks)]
    return lax.ppermute(value, ("wide", "blk"), pairs)


def kernel_call(body, out_shape, operands, limit=VMEM_LIMIT, **kw):
    return pl.pallas_call(
        body, out_shape=out_shape, compiler_params=pltpu.CompilerParams(vmem_limit_bytes=limit), **kw
    )(*operands)


def pieces(value, count=3):
    out = []
    for _ in range(count - 1):
        top = value.astype(jnp.bfloat16)
        out.append(top)
        value = value - top.astype(jnp.float32)
    out.append(value.astype(jnp.bfloat16))
    return out


def dot(a, b, ca, cb, precision=None):
    return lax.dot_general(
        a, b, (((ca,), (cb,)), ((), ())), precision=precision, preferred_element_type=jnp.float32
    )


def pack_body(*refs):
    sources, (left, right), held, sems = refs[:8], refs[8:10], refs[10:18], refs[18]
    copies = [pltpu.make_async_copy(a, b, sems.at[i]) for i, (a, b) in enumerate(zip(sources, held))]
    for copy in copies:
        copy.start()
    mu, lp, lv, lam, rp, rv, col, w = held
    left[K + 2 :, :] = jnp.zeros((left.shape[0] - K - 2, LANES), jnp.float32)
    right[K + 4 :, :] = jnp.zeros((right.shape[0] - K - 4, right.shape[1]), jnp.float32)
    for copy in copies:
        copy.wait()
    left[:K, :] = lv[...].astype(jnp.float32)
    left[K : K + 1, :] = mu[...]
    left[K + 1 : K + 2, :] = lp[...].astype(jnp.float32)
    right[:K, :] = rv[...].astype(jnp.float32)
    weights = w[...].astype(jnp.float32)
    for s in range(lam.shape[0]):
        lanes = pl.ds(s * LANES, LANES)
        right[K : K + 1, lanes] = lam[s : s + 1, :]
        right[K + 1 : K + 2, lanes] = rp[s : s + 1, :].astype(jnp.float32)
        right[K + 2 : K + 3, lanes] = col[s : s + 1, :].astype(jnp.float32)
        right[K + 3 : K + 4, lanes] = weights[s : s + 1, :]


def left_side(left):
    index = lax.broadcasted_iota(jnp.int32, (K, LANES), 0).astype(jnp.float32)
    hot = jnp.where(left[K + 1 : K + 2, :] == index, -1.0, 0.0)
    side = jnp.concatenate([left[:K, :], hot], axis=0).T.astype(jnp.bfloat16)
    return side, jnp.broadcast_to(left[K : K + 1, :], (LANES, LANES)).T


def right_side(right):
    index = lax.broadcasted_iota(jnp.int32, (K, right.shape[1]), 0).astype(jnp.float32)
    pick = jnp.where(right[K + 1 : K + 2, :] == index, 1.0, 0.0)
    table = jnp.concatenate([pick, right[:K, :]], axis=0).astype(jnp.bfloat16)
    return table, jnp.where(right[K + 2 : K + 3, :] == index, right[K + 3 : K + 4, :], 0.0).astype(jnp.bfloat16)


def sketch_terms(side, freq, table, omega, lam):
    scale = jnp.concatenate([freq] * (lam.shape[1] // LANES), axis=1) - lam
    loewner = dot(side, table, 1, 0) / scale
    return sum(dot(piece, omega, 1, 1) for piece in pieces(loewner))


def local_body(*refs):
    lefts, (right, side_out, freq_out, table_out, omega_out, total, cross) = refs[:-7], refs[-7:]
    table, omega = right_side(right)
    table_out[...] = table
    omega_out[...] = omega
    for q, left in enumerate(lefts):
        span = slice(q * LANES, (q + 1) * LANES)
        side, freq = left_side(left)
        side_out[span, :] = side
        freq_out[span, :] = freq
        total[span, :] = sketch_terms(side, freq, table, omega, right[K : K + 1, :])
    cross[...] = dot(omega, table[K:, :], 1, 1)


def sketch_body(distance, *refs):
    count = (len(refs) - 11) // 2
    owns, gots = refs[:count], refs[count : 2 * count]
    right, other, side_in, freq_in, table_in, omega_in, total_in, cross_in, pay, freq_row, port_row = refs[2 * count :]
    table, omega = right_side(other)
    near, far = right[K : K + 1, :], other[K : K + 1, :]
    here = lax.rem(lax.div(lax.axis_index("blk"), distance), 2) == 0
    for q in range(count):
        span = slice(q * LANES, (q + 1) * LANES)
        side, freq = left_side(gots[q])
        both = sketch_terms(
            jnp.concatenate([side_in[span, :], side], axis=0), jnp.concatenate([freq_in[span, :], freq], axis=0), table, omega, far
        )
        own = (both[:LANES, :] + total_in[span, :]).T
        got = (both[LANES:, :] + sketch_terms(side, freq, table_in[...], omega_in[...], near)).T
        for place, flip in ((q, False), (count + q, True)):
            spot = slice(place * K, (place + 1) * K)
            pay[spot, :] = jnp.where(here != flip, own, got)
            for out, row in ((freq_row, K), (port_row, K + 1)):
                out[place : place + 1, :] = jnp.where(here != flip, owns[q][row : row + 1, :], gots[q][row : row + 1, :])
    cross = cross_in[...] + dot(omega, table[K:, :], 1, 1)
    pay[2 * count * K :, :] = jnp.concatenate([cross[: K // 2], cross[K // 2 :]], axis=1)


def moments_body(own, other, freq, ports, gc, full):
    n_left = freq.shape[0]
    both = own[...] + other[...]
    index = lax.broadcasted_iota(jnp.int32, (K, LANES), 0).astype(jnp.float32)
    cross = both[n_left * K :, :]
    cross = pieces(jnp.concatenate([cross[:, :K], cross[:, K:]], axis=0))
    sketches, shifts = [], []
    for q in range(n_left):
        sketch = both[q * K : (q + 1) * K, :]
        hot = jnp.where(ports[q : q + 1, :] == index, 1.0, 0.0).astype(jnp.bfloat16)
        shift = freq[q : q + 1, :] * sketch
        for piece in cross:
            shift = shift + dot(piece, hot, 1, 0)
        sketches.append(sketch)
        shifts.append(shift)
    sketch = jnp.concatenate(sketches, axis=1)
    gc[...] = dot(sketch, jnp.concatenate([sketch, jnp.concatenate(shifts, axis=1)], axis=0), 1, 1, HIGHEST)
    full[...] = both[: n_left * K, :]


def full(value):
    return jnp.broadcast_to(value, (SUB, LANES))


def inverse_factor(gram, spread):
    lane = lax.broadcasted_iota(jnp.int32, (SUB, LANES), 1)
    sub = lax.broadcasted_iota(jnp.int32, (SUB, LANES), 0)
    count = K // SUB
    blocks = [
        jnp.where(lane < K, gram[r * SUB : (r + 1) * SUB, :], jnp.where(lane == sub + (K + r * SUB), 1.0, 0.0))
        for r in range(count)
    ]
    out = []
    for r in range(count):
        here, first, base = blocks[r], r * SUB, r * SUB * (SUB + 1)
        below = range(r + 1, count)
        for u in range(SUB):
            spread[base + u * SUB : base + (u + 1) * SUB, :] = full(here[:, first + u : first + u + 1])
        last = base + SUB * SUB
        spread[last : last + SUB, :] = here
        part = {(t, u): full(spread[base + u * SUB + t : base + u * SUB + t + 1, :]) for t in range(SUB) for u in range(t + 1)}
        rows = [full(spread[last + t : last + t + 1, :]) for t in range(SUB)]
        cols = {q: [full(blocks[q][:, first + u : first + u + 1]) for u in range(SUB)] for q in below}
        inverse = []
        for u in range(SUB):
            inverse.append(1.0 / part[u, u])
            ratio = {t: part[t, u] * inverse[u] for t in range(u + 1, SUB)}
            for t in range(u + 1, SUB):
                for v in range(u + 1, t + 1):
                    if t == u + 1:
                        part[t, v] = part[t, v] - (part[t, u] * part[v, u]) * inverse[u]
                    else:
                        part[t, v] = part[t, v] - ratio[t] * part[v, u]
            for t in range(u + 1, SUB):
                rows[t] = rows[t] - ratio[t] * rows[u]
                for q in below:
                    cols[q][t] = cols[q][t] - ratio[t] * cols[q][u]
        done, pivot = rows[0], part[0, 0]
        for t in range(1, SUB):
            done, pivot = jnp.where(sub == t, rows[t], done), jnp.where(sub == t, part[t, t], pivot)
        out.append((done * lax.rsqrt(pivot))[:, K:])
        rows = [row * inv for row, inv in zip(rows, inverse)]
        for q in below:
            terms = [col * row for col, row in zip(cols[q], rows)]
            while len(terms) > 1:
                terms = [a + b for a, b in zip(terms[::2], terms[1::2])]
            blocks[q] = blocks[q] - terms[0]
    return jnp.concatenate(out, axis=0)


def finish_body(scale, own, first, second, third, sketch, basis, projected, spread):
    gc = ((own[...] + first[...]) + (second[...] + third[...])) * scale
    inverse = inverse_factor(gc, spread)
    mine = pl.multiple_of(lax.div(lax.axis_index("blk"), 2) * K, K)
    basis[...] = dot(inverse, sketch[pl.ds(mine, K), :], 1, 0, HIGHEST)
    coefficient = dot(inverse, gc[:, K:], 1, 0, HIGHEST)
    projected[...] = dot(inverse, coefficient, 0, 0, HIGHEST)


def per_device(left_points, left_ports, left_values, right_points, right_ports, right_values, sketch_block, sketch_weight):
    f32 = jnp.float32
    rows, rights = left_points.shape[0], right_points.shape[0]
    blk, wide = lax.axis_size("blk"), lax.axis_size("wide")
    along = (rights // LANES, LANES)
    left, right = kernel_call(
        pack_body,
        (jax.ShapeDtypeStruct((K + SUB, LANES), f32), jax.ShapeDtypeStruct((K + SUB, rights), f32)),
        tuple(pltpu.with_memory_space_constraint(v, pltpu.HBM) for v in (
            left_points.reshape(1, rows),
            left_ports.reshape(1, rows),
            left_values.T,
            right_points.reshape(along),
            right_ports.reshape(along),
            right_values.T,
            sketch_block.reshape(along),
            sketch_weight.reshape(along),
        )),
        in_specs=[pl.BlockSpec(memory_space=pltpu.HBM)] * 8,
        scratch_shapes=[
            pltpu.VMEM((1, rows), f32),
            pltpu.VMEM((1, rows), jnp.int32),
            pltpu.VMEM((K, rows), left_values.dtype),
            pltpu.VMEM(along, f32),
            pltpu.VMEM(along, jnp.int32),
            pltpu.VMEM((K, rights), right_values.dtype),
            pltpu.VMEM(along, jnp.int32),
            pltpu.VMEM(along, sketch_weight.dtype),
            pltpu.SemaphoreType.DMA((8,)),
        ],
    )
    place = lax.axis_index("blk")
    lefts, distance = [left], 2
    while True:
        got = [swap(v, distance) for v in lefts]
        if distance * 2 >= blk:
            break
        here = (place // distance) % 2 == 0
        lefts = [jnp.where(here, a, b) for a, b in zip(lefts, got)] + [jnp.where(here, b, a) for a, b in zip(lefts, got)]
        distance *= 2
    other = swap(right, 1)
    count = len(lefts)
    held = 2 * count
    local = kernel_call(
        local_body,
        (
            jax.ShapeDtypeStruct((count * LANES, LANES), jnp.bfloat16),
            jax.ShapeDtypeStruct((count * LANES, LANES), f32),
            jax.ShapeDtypeStruct((2 * K, rights), jnp.bfloat16),
            jax.ShapeDtypeStruct((K, rights), jnp.bfloat16),
            jax.ShapeDtypeStruct((count * LANES, K), f32),
            jax.ShapeDtypeStruct((K, K), f32),
        ),
        (*lefts, right),
    )
    pay, freq, ports = kernel_call(
        functools.partial(sketch_body, distance),
        (
            jax.ShapeDtypeStruct((held * K + K // 2, LANES), f32),
            jax.ShapeDtypeStruct((held, LANES), f32),
            jax.ShapeDtypeStruct((held, LANES), f32),
        ),
        (*lefts, *got, right, other, *local),
    )
    step = 2
    while step < distance:
        pay = pay + swap(pay, step)
        step *= 2
    gc, sketch = kernel_call(
        moments_body,
        (jax.ShapeDtypeStruct((K, LANES), f32), jax.ShapeDtypeStruct((held * K, LANES), f32)),
        (pay, swap(pay, distance), freq, ports),
    )
    gc = gc + swap(gc, 0, 1)
    hops, distance = [(1, 1)], 2
    while distance < wide:
        hops.append((0, distance + 1))
        distance *= 2
    for hop in hops[:-2]:
        gc = gc + swap(gc, *hop)
    (b0, w0), (b1, w1) = hops[-2:]
    parts = (gc, swap(gc, b0, w0), swap(gc, b1, w1), swap(gc, b0 ^ b1, w0 ^ w1 ^ 1))
    basis, projected = kernel_call(
        functools.partial(finish_body, 1.0 / (rows * blk * wide)),
        (jax.ShapeDtypeStruct((K, rows), f32), jax.ShapeDtypeStruct((K, K), f32)),
        (*parts, sketch),
        scratch_shapes=[pltpu.VMEM((K * (SUB + 1), LANES), f32)],
    )
    return basis.T, projected


def solution(mesh):
    split = P(("wide", "blk"))
    return jax.shard_map(
        per_device,
        mesh=mesh,
        in_specs=(split, split, P(("wide", "blk"), None), P("blk"), P("blk"), P("blk", None), P("blk"), P("blk")),
        out_specs=(P(("wide", "blk"), None), P()),
        check_vma=False,
    )
```

```python
import functools

import jax
import jax.numpy as jnp
from jax import lax
from jax.experimental import pallas as pl
from jax.experimental.pallas import tpu as pltpu
from jax.sharding import PartitionSpec as P

K = 64
LANES = 128
SUB = 8
HIGHEST = lax.Precision.HIGHEST
VMEM_LIMIT = 8 << 20


def swap(value, blk=0, wide=0):
    wides, blks = lax.axis_size("wide"), lax.axis_size("blk")
    pairs = [(w * blks + b, (w ^ wide) * blks + (b ^ blk)) for w in range(wides) for b in range(blks)]
    return lax.ppermute(value, ("wide", "blk"), pairs)


def kernel_call(body, out_shape, operands, limit=VMEM_LIMIT, **kw):
    return pl.pallas_call(
        body, out_shape=out_shape, compiler_params=pltpu.CompilerParams(vmem_limit_bytes=limit), **kw
    )(*operands)


def pieces(value, count=3):
    out = []
    for _ in range(count - 1):
        top = value.astype(jnp.bfloat16)
        out.append(top)
        value = value - top.astype(jnp.float32)
    out.append(value.astype(jnp.bfloat16))
    return out


def dot(a, b, ca, cb, precision=None):
    return lax.dot_general(
        a, b, (((ca,), (cb,)), ((), ())), precision=precision, preferred_element_type=jnp.float32
    )


def pack_body(*refs):
    sources, (left, right), held, sems = refs[:8], refs[8:10], refs[10:18], refs[18]
    copies = [pltpu.make_async_copy(a, b, sems.at[i]) for i, (a, b) in enumerate(zip(sources, held))]
    for copy in copies:
        copy.start()
    mu, lp, lv, lam, rp, rv, col, w = held
    left[K + 2 :, :] = jnp.zeros((left.shape[0] - K - 2, LANES), jnp.float32)
    right[K + 4 :, :] = jnp.zeros((right.shape[0] - K - 4, right.shape[1]), jnp.float32)
    for copy in copies:
        copy.wait()
    left[:K, :] = lv[...].astype(jnp.float32)
    left[K : K + 1, :] = mu[...]
    left[K + 1 : K + 2, :] = lp[...].astype(jnp.float32)
    right[:K, :] = rv[...].astype(jnp.float32)
    weights = w[...].astype(jnp.float32)
    for s in range(lam.shape[0]):
        lanes = pl.ds(s * LANES, LANES)
        right[K : K + 1, lanes] = lam[s : s + 1, :]
        right[K + 1 : K + 2, lanes] = rp[s : s + 1, :].astype(jnp.float32)
        right[K + 2 : K + 3, lanes] = col[s : s + 1, :].astype(jnp.float32)
        right[K + 3 : K + 4, lanes] = weights[s : s + 1, :]


def left_side(left):
    index = lax.broadcasted_iota(jnp.int32, (K, LANES), 0).astype(jnp.float32)
    hot = jnp.where(left[K + 1 : K + 2, :] == index, -1.0, 0.0)
    side = jnp.concatenate([left[:K, :], hot], axis=0).T.astype(jnp.bfloat16)
    return side, jnp.broadcast_to(left[K : K + 1, :], (LANES, LANES)).T


def right_side(right):
    index = lax.broadcasted_iota(jnp.int32, (K, right.shape[1]), 0).astype(jnp.float32)
    pick = jnp.where(right[K + 1 : K + 2, :] == index, 1.0, 0.0)
    table = jnp.concatenate([pick, right[:K, :]], axis=0).astype(jnp.bfloat16)
    return table, jnp.where(right[K + 2 : K + 3, :] == index, right[K + 3 : K + 4, :], 0.0).astype(jnp.bfloat16)


def sketch_terms(side, freq, table, omega, lam):
    scale = jnp.concatenate([freq] * (lam.shape[1] // LANES), axis=1) - lam
    loewner = dot(side, table, 1, 0) / scale
    terms = dot(jnp.concatenate(pieces(loewner), axis=0), omega, 1, 1)
    return sum(jnp.split(terms, 3, axis=0))


def local_body(*refs):
    lefts, (right, side_out, freq_out, table_out, omega_out, total, cross) = refs[:-7], refs[-7:]
    table, omega = right_side(right)
    table_out[...] = table
    omega_out[...] = omega
    for q, left in enumerate(lefts):
        span = slice(q * LANES, (q + 1) * LANES)
        side, freq = left_side(left)
        side_out[span, :] = side
        freq_out[span, :] = freq
        total[span, :] = sketch_terms(side, freq, table, omega, right[K : K + 1, :])
    cross[...] = dot(omega, table[K:, :], 1, 1)


def remote_body(*refs):
    side, freq, right, total_in, cross_in, table_out, omega_out, total, cross = refs
    table, omega = right_side(right)
    table_out[...] = table
    omega_out[...] = omega
    for q in range(side.shape[0] // LANES):
        span = slice(q * LANES, (q + 1) * LANES)
        total[span, :] = total_in[span, :] + sketch_terms(side[span, :], freq[span, :], table, omega, right[K : K + 1, :])
    cross[...] = cross_in[...] + dot(omega, table[K:, :], 1, 1)


def sketch_body(distance, *refs):
    count = (len(refs) - 11) // 2
    owns, gots = refs[:count], refs[count : 2 * count]
    near, far, near_table, near_omega, far_table, far_omega, total, cross, pay, freq_row, port_row = refs[2 * count :]
    table = jnp.concatenate([near_table[...], far_table[...]], axis=1)
    omega = jnp.concatenate([near_omega[...], far_omega[...]], axis=1)
    lam = jnp.concatenate([near[K : K + 1, :], far[K : K + 1, :]], axis=1)
    here = lax.rem(lax.div(lax.axis_index("blk"), distance), 2) == 0
    for q in range(count):
        own = total[q * LANES : (q + 1) * LANES, :].T
        got = sketch_terms(*left_side(gots[q]), table, omega, lam).T
        for place, flip in ((q, False), (count + q, True)):
            spot = slice(place * K, (place + 1) * K)
            pay[spot, :] = jnp.where(here != flip, own, got)
            for out, row in ((freq_row, K), (port_row, K + 1)):
                out[place : place + 1, :] = jnp.where(here != flip, owns[q][row : row + 1, :], gots[q][row : row + 1, :])
    pay[2 * count * K :, :] = jnp.concatenate([cross[: K // 2, :], cross[K // 2 :, :]], axis=1)


def moments_body(own, other, freq, ports, gc, full):
    n_left = freq.shape[0]
    both = own[...] + other[...]
    index = lax.broadcasted_iota(jnp.int32, (K, LANES), 0).astype(jnp.float32)
    cross = both[n_left * K :, :]
    cross = pieces(jnp.concatenate([cross[:, :K], cross[:, K:]], axis=0))
    sketches, shifts = [], []
    for q in range(n_left):
        sketch = both[q * K : (q + 1) * K, :]
        hot = jnp.where(ports[q : q + 1, :] == index, 1.0, 0.0).astype(jnp.bfloat16)
        shift = freq[q : q + 1, :] * sketch
        for piece in cross:
            shift = shift + dot(piece, hot, 1, 0)
        sketches.append(sketch)
        shifts.append(shift)
    sketch = jnp.concatenate(sketches, axis=1)
    gc[...] = dot(sketch, jnp.concatenate([sketch, jnp.concatenate(shifts, axis=1)], axis=0), 1, 1, HIGHEST)
    full[...] = both[: n_left * K, :]


def full(value):
    return jnp.broadcast_to(value, (SUB, LANES))


def inverse_factor(gram, spread):
    lane = lax.broadcasted_iota(jnp.int32, (SUB, LANES), 1)
    sub = lax.broadcasted_iota(jnp.int32, (SUB, LANES), 0)
    count = K // SUB
    blocks = [
        jnp.where(lane < K, gram[r * SUB : (r + 1) * SUB, :], jnp.where(lane == sub + (K + r * SUB), 1.0, 0.0))
        for r in range(count)
    ]
    out = []
    for r in range(count):
        here, first, base = blocks[r], r * SUB, r * SUB * (SUB + 1)
        below = range(r + 1, count)
        for u in range(SUB):
            spread[base + u * SUB : base + (u + 1) * SUB, :] = full(here[:, first + u : first + u + 1])
        last = base + SUB * SUB
        spread[last : last + SUB, :] = here
        part = {(t, u): full(spread[base + u * SUB + t : base + u * SUB + t + 1, :]) for t in range(SUB) for u in range(t + 1)}
        rows = [full(spread[last + t : last + t + 1, :]) for t in range(SUB)]
        cols = {q: [full(blocks[q][:, first + u : first + u + 1]) for u in range(SUB)] for q in below}
        inverse = []
        for u in range(SUB):
            inverse.append(1.0 / part[u, u])
            ratio = {t: part[t, u] * inverse[u] for t in range(u + 1, SUB)}
            for t in range(u + 1, SUB):
                for v in range(u + 1, t + 1):
                    if t == u + 1:
                        part[t, v] = part[t, v] - (part[t, u] * part[v, u]) * inverse[u]
                    else:
                        part[t, v] = part[t, v] - ratio[t] * part[v, u]
            for t in range(u + 1, SUB):
                rows[t] = rows[t] - ratio[t] * rows[u]
                for q in below:
                    cols[q][t] = cols[q][t] - ratio[t] * cols[q][u]
        done, pivot = rows[0], part[0, 0]
        for t in range(1, SUB):
            done, pivot = jnp.where(sub == t, rows[t], done), jnp.where(sub == t, part[t, t], pivot)
        out.append((done * lax.rsqrt(pivot))[:, K:])
        rows = [row * inv for row, inv in zip(rows, inverse)]
        for q in below:
            terms = [col * row for col, row in zip(cols[q], rows)]
            while len(terms) > 1:
                terms = [a + b for a, b in zip(terms[::2], terms[1::2])]
            blocks[q] = blocks[q] - terms[0]
    return jnp.concatenate(out, axis=0)


def finish_body(scale, own, first, second, third, sketch, basis, projected, spread):
    gc = ((own[...] + first[...]) + (second[...] + third[...])) * scale
    inverse = inverse_factor(gc, spread)
    mine = pl.multiple_of(lax.div(lax.axis_index("blk"), 2) * K, K)
    both = dot(inverse, jnp.concatenate([sketch[pl.ds(mine, K), :], gc[:, K:]], axis=1), 1, 0, HIGHEST)
    basis[...] = both[:, :LANES]
    projected[...] = dot(inverse, both[:, LANES:], 0, 0, HIGHEST)


def per_device(left_points, left_ports, left_values, right_points, right_ports, right_values, sketch_block, sketch_weight):
    f32 = jnp.float32
    rows, rights = left_points.shape[0], right_points.shape[0]
    blk, wide = lax.axis_size("blk"), lax.axis_size("wide")
    along = (rights // LANES, LANES)
    left, right = kernel_call(
        pack_body,
        (jax.ShapeDtypeStruct((K + SUB, LANES), f32), jax.ShapeDtypeStruct((K + SUB, rights), f32)),
        tuple(pltpu.with_memory_space_constraint(v, pltpu.HBM) for v in (
            left_points.reshape(1, rows),
            left_ports.reshape(1, rows),
            left_values.T,
            right_points.reshape(along),
            right_ports.reshape(along),
            right_values.T,
            sketch_block.reshape(along),
            sketch_weight.reshape(along),
        )),
        in_specs=[pl.BlockSpec(memory_space=pltpu.HBM)] * 8,
        scratch_shapes=[
            pltpu.VMEM((1, rows), f32),
            pltpu.VMEM((1, rows), jnp.int32),
            pltpu.VMEM((K, rows), left_values.dtype),
            pltpu.VMEM(along, f32),
            pltpu.VMEM(along, jnp.int32),
            pltpu.VMEM((K, rights), right_values.dtype),
            pltpu.VMEM(along, jnp.int32),
            pltpu.VMEM(along, sketch_weight.dtype),
            pltpu.SemaphoreType.DMA((8,)),
        ],
    )
    place = lax.axis_index("blk")
    lefts, distance = [left], 2
    while True:
        got = [swap(v, distance) for v in lefts]
        if distance * 2 >= blk:
            break
        here = (place // distance) % 2 == 0
        lefts = [jnp.where(here, a, b) for a, b in zip(lefts, got)] + [jnp.where(here, b, a) for a, b in zip(lefts, got)]
        distance *= 2
    other = swap(right, 1)
    count = len(lefts)
    held = 2 * count
    local = kernel_call(
        local_body,
        (
            jax.ShapeDtypeStruct((count * LANES, LANES), jnp.bfloat16),
            jax.ShapeDtypeStruct((count * LANES, LANES), f32),
            jax.ShapeDtypeStruct((2 * K, rights), jnp.bfloat16),
            jax.ShapeDtypeStruct((K, rights), jnp.bfloat16),
            jax.ShapeDtypeStruct((count * LANES, K), f32),
            jax.ShapeDtypeStruct((K, K), f32),
        ),
        (*lefts, right),
    )
    side, freq, table, omega, total, cross = local
    far_table, far_omega, total, cross = kernel_call(
        remote_body,
        (
            jax.ShapeDtypeStruct(table.shape, table.dtype),
            jax.ShapeDtypeStruct(omega.shape, omega.dtype),
            jax.ShapeDtypeStruct(total.shape, f32),
            jax.ShapeDtypeStruct(cross.shape, f32),
        ),
        (side, freq, other, total, cross),
    )
    pay, freq, ports = kernel_call(
        functools.partial(sketch_body, distance),
        (
            jax.ShapeDtypeStruct((held * K + K // 2, LANES), f32),
            jax.ShapeDtypeStruct((held, LANES), f32),
            jax.ShapeDtypeStruct((held, LANES), f32),
        ),
        (*lefts, *got, right, other, table, omega, far_table, far_omega, total, cross),
    )
    step = 2
    while step < distance:
        pay = pay + swap(pay, step)
        step *= 2
    gc, sketch = kernel_call(
        moments_body,
        (jax.ShapeDtypeStruct((K, LANES), f32), jax.ShapeDtypeStruct((held * K, LANES), f32)),
        (pay, swap(pay, distance), freq, ports),
    )
    gc = gc + swap(gc, 0, 1)
    hops, distance = [(1, 1)], 2
    while distance < wide:
        hops.append((0, distance + 1))
        distance *= 2
    for hop in hops[:-2]:
        gc = gc + swap(gc, *hop)
    (b0, w0), (b1, w1) = hops[-2:]
    parts = [gc]
    for b, w in ((b0, w0), (b1, w1), (b0 ^ b1, w0 ^ w1 ^ 1)):
        parts.append(swap(gc, b, w))
    basis, projected = kernel_call(
        functools.partial(finish_body, 1.0 / (rows * blk * wide)),
        (jax.ShapeDtypeStruct((K, rows), f32), jax.ShapeDtypeStruct((K, K), f32)),
        (*parts, sketch),
        scratch_shapes=[pltpu.VMEM((K * (SUB + 1), LANES), f32)],
    )
    return basis.T, projected


def solution(mesh):
    split = P(("wide", "blk"))
    return jax.shard_map(
        per_device,
        mesh=mesh,
        in_specs=(split, split, P(("wide", "blk"), None), P("blk"), P("blk"), P("blk", None), P("blk"), P("blk")),
        out_specs=(P(("wide", "blk"), None), P()),
        check_vma=False,
    )
```

```python
import functools

import jax
import jax.numpy as jnp
from jax import lax
from jax.experimental import pallas as pl
from jax.experimental.pallas import tpu as pltpu
from jax.sharding import PartitionSpec as P

K = 64
LANES = 128
SUB = 8
HIGHEST = lax.Precision.HIGHEST
VMEM_LIMIT = 8 << 20


def swap(value, blk=0, wide=0):
    wides, blks = lax.axis_size("wide"), lax.axis_size("blk")
    pairs = [(w * blks + b, (w ^ wide) * blks + (b ^ blk)) for w in range(wides) for b in range(blks)]
    return lax.ppermute(value, ("wide", "blk"), pairs)


def kernel_call(body, out_shape, operands, limit=VMEM_LIMIT, **kw):
    return pl.pallas_call(
        body, out_shape=out_shape, compiler_params=pltpu.CompilerParams(vmem_limit_bytes=limit), **kw
    )(*operands)


def pieces(value, count=3):
    out = []
    for _ in range(count - 1):
        top = value.astype(jnp.bfloat16)
        out.append(top)
        value = value - top.astype(jnp.float32)
    out.append(value.astype(jnp.bfloat16))
    return out


def dot(a, b, ca, cb, precision=None):
    return lax.dot_general(
        a, b, (((ca,), (cb,)), ((), ())), precision=precision, preferred_element_type=jnp.float32
    )


def pack_body(*refs):
    sources, (left, right), held, sems = refs[:8], refs[8:10], refs[10:18], refs[18]
    copies = [pltpu.make_async_copy(a, b, sems.at[i]) for i, (a, b) in enumerate(zip(sources, held))]
    for i in (5, 2, 0, 1, 3, 4, 6, 7):
        copies[i].start()
    mu, lp, lv, lam, rp, rv, col, w = held
    left[K + 2 :, :] = jnp.zeros((left.shape[0] - K - 2, LANES), jnp.float32)
    for copy in copies:
        copy.wait()
    left[:K, :] = lv[...].astype(jnp.float32)
    left[K : K + 1, :] = mu[...]
    left[K + 1 : K + 2, :] = lp[...].astype(jnp.float32)
    count = lam.shape[0]
    for s in range(count):
        right[s * K : (s + 1) * K, :] = rv[:, s * LANES : (s + 1) * LANES].astype(jnp.float32)
    for place, rows in enumerate((lam, rp, col, w)):
        right[count * K + place * count : count * K + (place + 1) * count, :] = rows[...].astype(jnp.float32)


def of_right(right):
    count = right.shape[0] // (K + 4)
    values = jnp.concatenate([right[s * K : (s + 1) * K, :] for s in range(count)], axis=1)
    rows = [jnp.concatenate([right[count * K + p * count + s : count * K + p * count + s + 1, :] for s in range(count)], axis=1) for p in range(4)]
    return values, *rows


def left_side(left):
    index = lax.broadcasted_iota(jnp.int32, (K, LANES), 0).astype(jnp.float32)
    hot = jnp.where(left[K + 1 : K + 2, :] == index, -1.0, 0.0)
    side = jnp.concatenate([left[:K, :], hot], axis=0).T.astype(jnp.bfloat16)
    return side, jnp.broadcast_to(left[K : K + 1, :], (LANES, LANES)).T


def right_side(right):
    values, lam, ports, columns, weights = of_right(right)
    index = lax.broadcasted_iota(jnp.int32, values.shape, 0).astype(jnp.float32)
    table = jnp.concatenate([jnp.where(ports == index, 1.0, 0.0), values], axis=0).astype(jnp.bfloat16)
    return table, jnp.where(columns == index, weights, 0.0).astype(jnp.bfloat16), lam


def sketch_terms(side, freq, table, omega, lam):
    scale = jnp.concatenate([freq] * (lam.shape[1] // LANES), axis=1) - lam
    loewner = dot(side, table, 1, 0) / scale
    terms = dot(jnp.concatenate(pieces(loewner), axis=0), omega, 1, 1)
    return sum(jnp.split(terms, 3, axis=0))


def local_body(*refs):
    lefts, (right, side_out, freq_out, table_out, omega_out, total, cross) = refs[:-7], refs[-7:]
    table, omega, lam = right_side(right)
    table_out[...] = table
    omega_out[...] = omega
    for q, left in enumerate(lefts):
        span = slice(q * LANES, (q + 1) * LANES)
        side, freq = left_side(left)
        side_out[span, :] = side
        freq_out[span, :] = freq
        total[span, :] = sketch_terms(side, freq, table, omega, lam)
    cross[...] = dot(omega, table[K:, :], 1, 1)


def remote_body(*refs):
    side, freq, right, total_in, cross_in, table_out, omega_out, total, cross = refs
    table, omega, lam = right_side(right)
    table_out[...] = table
    omega_out[...] = omega
    for q in range(side.shape[0] // LANES):
        span = slice(q * LANES, (q + 1) * LANES)
        total[span, :] = total_in[span, :] + sketch_terms(side[span, :], freq[span, :], table, omega, lam)
    cross[...] = cross_in[...] + dot(omega, table[K:, :], 1, 1)


def sketch_body(distance, *refs):
    count = (len(refs) - 11) // 2
    owns, gots = refs[:count], refs[count : 2 * count]
    near, far, near_table, near_omega, far_table, far_omega, total, cross, pay, freq_row, port_row = refs[2 * count :]
    table = jnp.concatenate([near_table[...], far_table[...]], axis=1)
    omega = jnp.concatenate([near_omega[...], far_omega[...]], axis=1)
    lam = jnp.concatenate([of_right(near)[1], of_right(far)[1]], axis=1)
    here = lax.rem(lax.div(lax.axis_index("blk"), distance), 2) == 0
    for q in range(count):
        own = total[q * LANES : (q + 1) * LANES, :].T
        got = sketch_terms(*left_side(gots[q]), table, omega, lam).T
        for place, flip in ((q, False), (count + q, True)):
            spot = slice(place * K, (place + 1) * K)
            pay[spot, :] = jnp.where(here != flip, own, got)
            for out, row in ((freq_row, K), (port_row, K + 1)):
                out[place : place + 1, :] = jnp.where(here != flip, owns[q][row : row + 1, :], gots[q][row : row + 1, :])
    pay[2 * count * K :, :] = jnp.concatenate([cross[: K // 2, :], cross[K // 2 :, :]], axis=1)


def moments_body(own, other, freq, ports, gc, full):
    n_left = freq.shape[0]
    both = own[...] + other[...]
    index = lax.broadcasted_iota(jnp.int32, (K, LANES), 0).astype(jnp.float32)
    cross = both[n_left * K :, :]
    cross = pieces(jnp.concatenate([cross[:, :K], cross[:, K:]], axis=0))
    sketches, shifts = [], []
    for q in range(n_left):
        sketch = both[q * K : (q + 1) * K, :]
        hot = jnp.where(ports[q : q + 1, :] == index, 1.0, 0.0).astype(jnp.bfloat16)
        shift = freq[q : q + 1, :] * sketch
        for piece in cross:
            shift = shift + dot(piece, hot, 1, 0)
        sketches.append(sketch)
        shifts.append(shift)
    sketch = jnp.concatenate(sketches, axis=1)
    gc[...] = dot(sketch, jnp.concatenate([sketch, jnp.concatenate(shifts, axis=1)], axis=0), 1, 1, HIGHEST)
    full[...] = both[: n_left * K, :]


def full(value):
    return jnp.broadcast_to(value, (SUB, LANES))


def inverse_factor(gram, spread):
    lane = lax.broadcasted_iota(jnp.int32, (SUB, LANES), 1)
    sub = lax.broadcasted_iota(jnp.int32, (SUB, LANES), 0)
    count = K // SUB
    blocks = [
        jnp.where(lane < K, gram[r * SUB : (r + 1) * SUB, :], jnp.where(lane == sub + (K + r * SUB), 1.0, 0.0))
        for r in range(count)
    ]
    out = []
    for r in range(count):
        here, first, base = blocks[r], r * SUB, r * SUB * (SUB + 1)
        below = range(r + 1, count)
        for u in range(SUB):
            spread[base + u * SUB : base + (u + 1) * SUB, :] = full(here[:, first + u : first + u + 1])
        last = base + SUB * SUB
        spread[last : last + SUB, :] = here
        part = {(t, u): full(spread[base + u * SUB + t : base + u * SUB + t + 1, :]) for t in range(SUB) for u in range(t + 1)}
        rows = [full(spread[last + t : last + t + 1, :]) for t in range(SUB)]
        cols = {q: [full(blocks[q][:, first + u : first + u + 1]) for u in range(SUB)] for q in below}
        inverse = []
        for u in range(SUB):
            inverse.append(1.0 / part[u, u])
            ratio = {t: part[t, u] * inverse[u] for t in range(u + 1, SUB)}
            for t in range(u + 1, SUB):
                for v in range(u + 1, t + 1):
                    if t == u + 1:
                        part[t, v] = part[t, v] - (part[t, u] * part[v, u]) * inverse[u]
                    else:
                        part[t, v] = part[t, v] - ratio[t] * part[v, u]
            for t in range(u + 1, SUB):
                rows[t] = rows[t] - ratio[t] * rows[u]
                for q in below:
                    cols[q][t] = cols[q][t] - ratio[t] * cols[q][u]
        done, pivot = rows[0], part[0, 0]
        for t in range(1, SUB):
            done, pivot = jnp.where(sub == t, rows[t], done), jnp.where(sub == t, part[t, t], pivot)
        out.append((done * lax.rsqrt(pivot))[:, K:])
        rows = [row * inv for row, inv in zip(rows, inverse)]
        for q in below:
            terms = [col * row for col, row in zip(cols[q], rows)]
            while len(terms) > 1:
                terms = [a + b for a, b in zip(terms[::2], terms[1::2])]
            blocks[q] = blocks[q] - terms[0]
    return jnp.concatenate(out, axis=0)


def finish_body(scale, own, first, second, third, sketch, basis, projected, spread):
    gc = ((own[...] + first[...]) + (second[...] + third[...])) * scale
    inverse = inverse_factor(gc, spread)
    mine = pl.multiple_of(lax.div(lax.axis_index("blk"), 2) * K, K)
    both = dot(inverse, jnp.concatenate([sketch[pl.ds(mine, K), :], gc[:, K:]], axis=1), 1, 0, HIGHEST)
    basis[...] = both[:, :LANES]
    projected[...] = dot(inverse, both[:, LANES:], 0, 0, HIGHEST)


def per_device(left_points, left_ports, left_values, right_points, right_ports, right_values, sketch_block, sketch_weight):
    f32 = jnp.float32
    rows, rights = left_points.shape[0], right_points.shape[0]
    blk, wide = lax.axis_size("blk"), lax.axis_size("wide")
    along = (rights // LANES, LANES)
    left, right = kernel_call(
        pack_body,
        (jax.ShapeDtypeStruct((K + SUB, LANES), f32), jax.ShapeDtypeStruct(((K + 4) * along[0], LANES), f32)),
        tuple(pltpu.with_memory_space_constraint(v, pltpu.HBM) for v in (
            left_points.reshape(1, rows),
            left_ports.reshape(1, rows),
            left_values.T,
            right_points.reshape(along),
            right_ports.reshape(along),
            right_values.T,
            sketch_block.reshape(along),
            sketch_weight.reshape(along),
        )),
        in_specs=[pl.BlockSpec(memory_space=pltpu.HBM)] * 8,
        scratch_shapes=[
            pltpu.VMEM((1, rows), f32),
            pltpu.VMEM((1, rows), jnp.int32),
            pltpu.VMEM((K, rows), left_values.dtype),
            pltpu.VMEM(along, f32),
            pltpu.VMEM(along, jnp.int32),
            pltpu.VMEM((K, rights), right_values.dtype),
            pltpu.VMEM(along, jnp.int32),
            pltpu.VMEM(along, sketch_weight.dtype),
            pltpu.SemaphoreType.DMA((8,)),
        ],
    )
    place = lax.axis_index("blk")
    lefts, distance = [left], 2
    while True:
        got = [swap(v, distance) for v in lefts]
        if distance * 2 >= blk:
            break
        here = (place // distance) % 2 == 0
        lefts = [jnp.where(here, a, b) for a, b in zip(lefts, got)] + [jnp.where(here, b, a) for a, b in zip(lefts, got)]
        distance *= 2
    other = swap(right, 1)
    count = len(lefts)
    held = 2 * count
    local = kernel_call(
        local_body,
        (
            jax.ShapeDtypeStruct((count * LANES, LANES), jnp.bfloat16),
            jax.ShapeDtypeStruct((count * LANES, LANES), f32),
            jax.ShapeDtypeStruct((2 * K, rights), jnp.bfloat16),
            jax.ShapeDtypeStruct((K, rights), jnp.bfloat16),
            jax.ShapeDtypeStruct((count * LANES, K), f32),
            jax.ShapeDtypeStruct((K, K), f32),
        ),
        (*lefts, right),
    )
    side, freq, table, omega, total, cross = local
    far_table, far_omega, total, cross = kernel_call(
        remote_body,
        (
            jax.ShapeDtypeStruct(table.shape, table.dtype),
            jax.ShapeDtypeStruct(omega.shape, omega.dtype),
            jax.ShapeDtypeStruct(total.shape, f32),
            jax.ShapeDtypeStruct(cross.shape, f32),
        ),
        (side, freq, other, total, cross),
    )
    pay, freq, ports = kernel_call(
        functools.partial(sketch_body, distance),
        (
            jax.ShapeDtypeStruct((held * K + K // 2, LANES), f32),
            jax.ShapeDtypeStruct((held, LANES), f32),
            jax.ShapeDtypeStruct((held, LANES), f32),
        ),
        (*lefts, *got, right, other, table, omega, far_table, far_omega, total, cross),
    )
    step = 2
    while step < distance:
        pay = pay + swap(pay, step)
        step *= 2
    gc, sketch = kernel_call(
        moments_body,
        (jax.ShapeDtypeStruct((K, LANES), f32), jax.ShapeDtypeStruct((held * K, LANES), f32)),
        (pay, swap(pay, distance), freq, ports),
    )
    gc = gc + swap(gc, 0, 1)
    hops, distance = [(1, 1)], 2
    while distance < wide:
        hops.append((0, distance + 1))
        distance *= 2
    for hop in hops[:-2]:
        gc = gc + swap(gc, *hop)
    (b0, w0), (b1, w1) = hops[-2:]
    parts = [gc]
    for b, w in ((b0, w0), (b1, w1), (b0 ^ b1, w0 ^ w1 ^ 1)):
        parts.append(swap(gc, b, w))
    basis, projected = kernel_call(
        functools.partial(finish_body, 1.0 / (rows * blk * wide)),
        (jax.ShapeDtypeStruct((K, rows), f32), jax.ShapeDtypeStruct((K, K), f32)),
        (*parts, sketch),
        scratch_shapes=[pltpu.VMEM((K * (SUB + 1), LANES), f32)],
    )
    return basis.T, projected


def solution(mesh):
    split = P(("wide", "blk"))
    return jax.shard_map(
        per_device,
        mesh=mesh,
        in_specs=(split, split, P(("wide", "blk"), None), P("blk"), P("blk"), P("blk", None), P("blk"), P("blk")),
        out_specs=(P(("wide", "blk"), None), P()),
        check_vma=False,
    )
```

```python
import functools

import jax
import jax.numpy as jnp
from jax import lax
from jax.experimental import pallas as pl
from jax.experimental.pallas import tpu as pltpu
from jax.sharding import PartitionSpec as P

K = 64
LANES = 128
SUB = 8
VMEM_LIMIT = 8 << 20


def swap(value, blk=0, wide=0):
    wides, blks = lax.axis_size("wide"), lax.axis_size("blk")
    pairs = [(w * blks + b, (w ^ wide) * blks + (b ^ blk)) for w in range(wides) for b in range(blks)]
    return lax.ppermute(value, ("wide", "blk"), pairs)


def kernel_call(body, out_shape, operands, limit=VMEM_LIMIT, **kw):
    return pl.pallas_call(
        body, out_shape=out_shape, compiler_params=pltpu.CompilerParams(vmem_limit_bytes=limit), **kw
    )(*operands)


def pieces(value, count=3):
    out = []
    for _ in range(count - 1):
        top = value.astype(jnp.bfloat16)
        out.append(top)
        value = value - top.astype(jnp.float32)
    out.append(value.astype(jnp.bfloat16))
    return out


def dot(a, b, ca, cb, precision=None):
    return lax.dot_general(
        a, b, (((ca,), (cb,)), ((), ())), precision=precision, preferred_element_type=jnp.float32
    )


def product(a, b):
    (h, m, l), (p, q, r) = pieces(a), pieces(b)
    return dot(jnp.concatenate([l, m, h, m, h, h], axis=1), jnp.concatenate([p, q, r, p, q, p], axis=0), 1, 0)


def pack_body(*refs):
    sources, (left, right), held, sems = refs[:8], refs[8:10], refs[10:18], refs[18]
    copies = [pltpu.make_async_copy(a, b, sems.at[i]) for i, (a, b) in enumerate(zip(sources, held))]
    for i in (5, 2, 0, 1, 3, 4, 6, 7):
        copies[i].start()
    mu, lp, lv, lam, rp, rv, col, w = held
    left[K + 2 :, :] = jnp.zeros((left.shape[0] - K - 2, LANES), jnp.float32)
    for copy in copies:
        copy.wait()
    left[:K, :] = lv[...].astype(jnp.float32)
    left[K : K + 1, :] = mu[...]
    left[K + 1 : K + 2, :] = lp[...].astype(jnp.float32)
    count = lam.shape[0]
    for s in range(count):
        right[s * K : (s + 1) * K, :] = rv[:, s * LANES : (s + 1) * LANES].astype(jnp.float32)
    for place, rows in enumerate((lam, rp, col, w)):
        right[count * K + place * count : count * K + (place + 1) * count, :] = rows[...].astype(jnp.float32)


def of_right(right):
    count = right.shape[0] // (K + 4)
    values = jnp.concatenate([right[s * K : (s + 1) * K, :] for s in range(count)], axis=1)
    rows = [jnp.concatenate([right[count * K + p * count + s : count * K + p * count + s + 1, :] for s in range(count)], axis=1) for p in range(4)]
    return values, *rows


def left_side(left):
    index = lax.broadcasted_iota(jnp.int32, (K, LANES), 0).astype(jnp.float32)
    hot = jnp.where(left[K + 1 : K + 2, :] == index, -1.0, 0.0)
    side = jnp.concatenate([left[:K, :], hot], axis=0).T.astype(jnp.bfloat16)
    return side, jnp.broadcast_to(left[K : K + 1, :], (LANES, LANES)).T


def right_side(right):
    values, lam, ports, columns, weights = of_right(right)
    index = lax.broadcasted_iota(jnp.int32, values.shape, 0).astype(jnp.float32)
    table = jnp.concatenate([jnp.where(ports == index, 1.0, 0.0), values], axis=0).astype(jnp.bfloat16)
    return table, jnp.where(columns == index, weights, 0.0).astype(jnp.bfloat16), lam


def sketch_terms(side, freq, table, omega, lam):
    scale = jnp.concatenate([freq] * (lam.shape[1] // LANES), axis=1) - lam
    loewner = dot(side, table, 1, 0) / scale
    terms = dot(omega, jnp.concatenate(pieces(loewner), axis=0), 1, 1)
    return sum(jnp.split(terms, 3, axis=1)[::-1])


def local_body(*refs):
    lefts, (right, side_out, freq_out, table_out, omega_out, total, cross) = refs[:-7], refs[-7:]
    table, omega, lam = right_side(right)
    table_out[...] = table
    omega_out[...] = omega
    for q, left in enumerate(lefts):
        span = slice(q * LANES, (q + 1) * LANES)
        side, freq = left_side(left)
        side_out[span, :] = side
        freq_out[span, :] = freq
        total[:, span] = sketch_terms(side, freq, table, omega, lam)
    cross[...] = dot(omega, table[K:, :], 1, 1)


def remote_body(*refs):
    side, freq, right, total_in, cross_in, table_out, omega_out, total, cross = refs
    table, omega, lam = right_side(right)
    table_out[...] = table
    omega_out[...] = omega
    for q in range(side.shape[0] // LANES):
        span = slice(q * LANES, (q + 1) * LANES)
        total[:, span] = total_in[:, span] + sketch_terms(side[span, :], freq[span, :], table, omega, lam)
    cross[...] = cross_in[...] + dot(omega, table[K:, :], 1, 1)


def sketch_body(distance, *refs):
    count = (len(refs) - 11) // 2
    owns, gots = refs[:count], refs[count : 2 * count]
    near, far, near_table, near_omega, far_table, far_omega, total, cross, pay, freq_row, port_row = refs[2 * count :]
    table = jnp.concatenate([near_table[...], far_table[...]], axis=1)
    omega = jnp.concatenate([near_omega[...], far_omega[...]], axis=1)
    lam = jnp.concatenate([of_right(near)[1], of_right(far)[1]], axis=1)
    here = lax.rem(lax.div(lax.axis_index("blk"), distance), 2) == 0
    for q in range(count):
        own = total[:, q * LANES : (q + 1) * LANES]
        got = sketch_terms(*left_side(gots[q]), table, omega, lam)
        for place, flip in ((q, False), (count + q, True)):
            spot = slice(place * K, (place + 1) * K)
            pay[spot, :] = jnp.where(here != flip, own, got)
            for out, row in ((freq_row, K), (port_row, K + 1)):
                out[place : place + 1, :] = jnp.where(here != flip, owns[q][row : row + 1, :], gots[q][row : row + 1, :])
    pay[2 * count * K :, :] = jnp.concatenate([cross[: K // 2, :], cross[K // 2 :, :]], axis=1)


def moments_body(own, other, freq, ports, gc, full):
    n_left = freq.shape[0]
    both = own[...] + other[...]
    index = lax.broadcasted_iota(jnp.int32, (K, LANES), 0).astype(jnp.float32)
    cross = both[n_left * K :, :]
    cross = pieces(jnp.concatenate([cross[:, :K], cross[:, K:]], axis=0))
    sketches, shifts = [], []
    for q in range(n_left):
        sketch = both[q * K : (q + 1) * K, :]
        hot = jnp.where(ports[q : q + 1, :] == index, 1.0, 0.0).astype(jnp.bfloat16)
        shift = freq[q : q + 1, :] * sketch
        for piece in cross:
            shift = shift + dot(piece, hot, 1, 0)
        sketches.append(sketch)
        shifts.append(shift)
    sketch = jnp.concatenate(sketches, axis=1)
    h, m, l = pieces(sketch)
    p, q, r = pieces(jnp.concatenate([sketch, jnp.concatenate(shifts, axis=1)], axis=0))
    terms = jnp.split(dot(jnp.concatenate([l, m, h], axis=0), p, 1, 1), 3, axis=0)
    terms += jnp.split(dot(jnp.concatenate([m, h], axis=0), q, 1, 1), 2, axis=0)
    low = (terms[0] + terms[3]) + dot(h, r, 1, 1)
    gc[...] = terms[2] + ((terms[1] + terms[4]) + low)
    full[...] = both[: n_left * K, :]


def full(value):
    return jnp.broadcast_to(value, (SUB, LANES))


def inverse_factor(gram, spread):
    lane = lax.broadcasted_iota(jnp.int32, (SUB, LANES), 1)
    sub = lax.broadcasted_iota(jnp.int32, (SUB, LANES), 0)
    count = K // SUB
    blocks = [
        jnp.where(lane < K, gram[r * SUB : (r + 1) * SUB, :], jnp.where(lane == sub + (K + r * SUB), 1.0, 0.0))
        for r in range(count)
    ]
    out = []
    for r in range(count):
        here, first, base = blocks[r], r * SUB, r * SUB * (SUB + 1)
        below = range(r + 1, count)
        for u in range(SUB):
            spread[base + u * SUB : base + (u + 1) * SUB, :] = full(here[:, first + u : first + u + 1])
        last = base + SUB * SUB
        spread[last : last + SUB, :] = here
        part = {(t, u): full(spread[base + u * SUB + t : base + u * SUB + t + 1, :]) for t in range(SUB) for u in range(t + 1)}
        rows = [full(spread[last + t : last + t + 1, :]) for t in range(SUB)]
        cols = {q: [full(blocks[q][:, first + u : first + u + 1]) for u in range(SUB)] for q in below}
        inverse = []
        for u in range(SUB):
            inverse.append(1.0 / part[u, u])
            ratio = {t: part[t, u] * inverse[u] for t in range(u + 1, SUB)}
            for t in range(u + 1, SUB):
                for v in range(u + 1, t + 1):
                    if t == u + 1:
                        part[t, v] = part[t, v] - (part[t, u] * part[v, u]) * inverse[u]
                    else:
                        part[t, v] = part[t, v] - ratio[t] * part[v, u]
            for t in range(u + 1, SUB):
                rows[t] = rows[t] - ratio[t] * rows[u]
                for q in below:
                    cols[q][t] = cols[q][t] - ratio[t] * cols[q][u]
        done, pivot = rows[0], part[0, 0]
        for t in range(1, SUB):
            done, pivot = jnp.where(sub == t, rows[t], done), jnp.where(sub == t, part[t, t], pivot)
        out.append((done * lax.rsqrt(pivot))[:, K:])
        rows = [row * inv for row, inv in zip(rows, inverse)]
        for q in below:
            terms = [col * row for col, row in zip(cols[q], rows)]
            while len(terms) > 1:
                terms = [a + b for a, b in zip(terms[::2], terms[1::2])]
            blocks[q] = blocks[q] - terms[0]
    return jnp.concatenate(out, axis=0)


def finish_body(scale, own, first, second, third, sketch, basis, projected, spread):
    gc = ((own[...] + first[...]) + (second[...] + third[...])) * scale
    inverse = inverse_factor(gc, spread)
    mine = pl.multiple_of(lax.div(lax.axis_index("blk"), 2) * K, K)
    both = product(inverse, jnp.concatenate([sketch[pl.ds(mine, K), :], gc[:, K:]], axis=1))
    basis[...] = both[:, :LANES]
    projected[...] = product(inverse.T, both[:, LANES:])


def per_device(left_points, left_ports, left_values, right_points, right_ports, right_values, sketch_block, sketch_weight):
    f32 = jnp.float32
    rows, rights = left_points.shape[0], right_points.shape[0]
    blk, wide = lax.axis_size("blk"), lax.axis_size("wide")
    along = (rights // LANES, LANES)
    left, right = kernel_call(
        pack_body,
        (jax.ShapeDtypeStruct((K + SUB, LANES), f32), jax.ShapeDtypeStruct(((K + 4) * along[0], LANES), f32)),
        tuple(pltpu.with_memory_space_constraint(v, pltpu.HBM) for v in (
            left_points.reshape(1, rows),
            left_ports.reshape(1, rows),
            left_values.T,
            right_points.reshape(along),
            right_ports.reshape(along),
            right_values.T,
            sketch_block.reshape(along),
            sketch_weight.reshape(along),
        )),
        in_specs=[pl.BlockSpec(memory_space=pltpu.HBM)] * 8,
        scratch_shapes=[
            pltpu.VMEM((1, rows), f32),
            pltpu.VMEM((1, rows), jnp.int32),
            pltpu.VMEM((K, rows), left_values.dtype),
            pltpu.VMEM(along, f32),
            pltpu.VMEM(along, jnp.int32),
            pltpu.VMEM((K, rights), right_values.dtype),
            pltpu.VMEM(along, jnp.int32),
            pltpu.VMEM(along, sketch_weight.dtype),
            pltpu.SemaphoreType.DMA((8,)),
        ],
    )
    place = lax.axis_index("blk")
    lefts, distance = [left], 2
    while True:
        got = [swap(v, distance) for v in lefts]
        if distance * 2 >= blk:
            break
        here = (place // distance) % 2 == 0
        lefts = [jnp.where(here, a, b) for a, b in zip(lefts, got)] + [jnp.where(here, b, a) for a, b in zip(lefts, got)]
        distance *= 2
    other = swap(right, 1)
    count = len(lefts)
    held = 2 * count
    local = kernel_call(
        local_body,
        (
            jax.ShapeDtypeStruct((count * LANES, LANES), jnp.bfloat16),
            jax.ShapeDtypeStruct((count * LANES, LANES), f32),
            jax.ShapeDtypeStruct((2 * K, rights), jnp.bfloat16),
            jax.ShapeDtypeStruct((K, rights), jnp.bfloat16),
            jax.ShapeDtypeStruct((K, count * LANES), f32),
            jax.ShapeDtypeStruct((K, K), f32),
        ),
        (*lefts, right),
    )
    side, freq, table, omega, total, cross = local
    far_table, far_omega, total, cross = kernel_call(
        remote_body,
        (
            jax.ShapeDtypeStruct(table.shape, table.dtype),
            jax.ShapeDtypeStruct(omega.shape, omega.dtype),
            jax.ShapeDtypeStruct(total.shape, f32),
            jax.ShapeDtypeStruct(cross.shape, f32),
        ),
        (side, freq, other, total, cross),
    )
    pay, freq, ports = kernel_call(
        functools.partial(sketch_body, distance),
        (
            jax.ShapeDtypeStruct((held * K + K // 2, LANES), f32),
            jax.ShapeDtypeStruct((held, LANES), f32),
            jax.ShapeDtypeStruct((held, LANES), f32),
        ),
        (*lefts, *got, right, other, table, omega, far_table, far_omega, total, cross),
    )
    step = 2
    while step < distance:
        pay = pay + swap(pay, step)
        step *= 2
    gc, sketch = kernel_call(
        moments_body,
        (jax.ShapeDtypeStruct((K, LANES), f32), jax.ShapeDtypeStruct((held * K, LANES), f32)),
        (pay, swap(pay, distance), freq, ports),
    )
    gc = gc + swap(gc, 0, 1)
    hops, distance = [(1, 1)], 2
    while distance < wide:
        hops.append((0, distance + 1))
        distance *= 2
    for hop in hops[:-2]:
        gc = gc + swap(gc, *hop)
    (b0, w0), (b1, w1) = hops[-2:]
    parts = [gc]
    for b, w in ((b0, w0), (b1, w1), (b0 ^ b1, w0 ^ w1 ^ 1)):
        parts.append(swap(gc, b, w))
    basis, projected = kernel_call(
        functools.partial(finish_body, 1.0 / (rows * blk * wide)),
        (jax.ShapeDtypeStruct((K, rows), f32), jax.ShapeDtypeStruct((K, K), f32)),
        (*parts, sketch),
        scratch_shapes=[pltpu.VMEM((K * (SUB + 1), LANES), f32)],
    )
    return basis.T, projected


def solution(mesh):
    split = P(("wide", "blk"))
    return jax.shard_map(
        per_device,
        mesh=mesh,
        in_specs=(split, split, P(("wide", "blk"), None), P("blk"), P("blk"), P("blk", None), P("blk"), P("blk")),
        out_specs=(P(("wide", "blk"), None), P()),
        check_vma=False,
    )
```

```python
import functools

import jax
import jax.numpy as jnp
from jax import lax
from jax.experimental import pallas as pl
from jax.experimental.pallas import tpu as pltpu
from jax.sharding import PartitionSpec as P

K = 64
LANES = 128
SUB = 8
VMEM_LIMIT = 8 << 20


def swap(value, blk=0, wide=0):
    wides, blks = lax.axis_size("wide"), lax.axis_size("blk")
    pairs = [(w * blks + b, (w ^ wide) * blks + (b ^ blk)) for w in range(wides) for b in range(blks)]
    return lax.ppermute(value, ("wide", "blk"), pairs)


def kernel_call(body, out_shape, operands, limit=VMEM_LIMIT, **kw):
    return pl.pallas_call(
        body, out_shape=out_shape, compiler_params=pltpu.CompilerParams(vmem_limit_bytes=limit), **kw
    )(*operands)


def pieces(value, count=3):
    out = []
    for _ in range(count - 1):
        top = value.astype(jnp.bfloat16)
        out.append(top)
        value = value - top.astype(jnp.float32)
    out.append(value.astype(jnp.bfloat16))
    return out


def dot(a, b, ca, cb, precision=None):
    return lax.dot_general(
        a, b, (((ca,), (cb,)), ((), ())), precision=precision, preferred_element_type=jnp.float32
    )


def product(a, b):
    (h, m, l), (p, q, r) = pieces(a), pieces(b)
    return dot(jnp.concatenate([l, m, h, m, h, h], axis=1), jnp.concatenate([p, q, r, p, q, p], axis=0), 1, 0)


def pack_body(*refs):
    sources, (left, right), held, sems = refs[:8], refs[8:10], refs[10:18], refs[18]
    copies = [pltpu.make_async_copy(a, b, sems.at[i]) for i, (a, b) in enumerate(zip(sources, held))]
    for i in (5, 2, 0, 1, 3, 4, 6, 7):
        copies[i].start()
    mu, lp, lv, lam, rp, rv, col, w = held
    for copy in copies:
        copy.wait()
    values = lv[...].astype(jnp.float32)
    for i in range(K // 2):
        left[i, :, :] = values[2 * i : 2 * i + 2, :]
    left[K // 2, :1, :] = mu[...]
    left[K // 2, 1:, :] = lp[...].astype(jnp.float32)
    count = lam.shape[0]
    for s in range(count):
        right[s * K : (s + 1) * K, :] = rv[:, s * LANES : (s + 1) * LANES].astype(jnp.float32)
    for place, rows in enumerate((lam, rp, col, w)):
        right[count * K + place * count : count * K + (place + 1) * count, :] = rows[...].astype(jnp.float32)


def of_right(right):
    count = right.shape[0] // (K + 4)
    values = jnp.concatenate([right[s * K : (s + 1) * K, :] for s in range(count)], axis=1)
    rows = [jnp.concatenate([right[count * K + p * count + s : count * K + p * count + s + 1, :] for s in range(count)], axis=1) for p in range(4)]
    return values, *rows


def left_side(left):
    index = lax.broadcasted_iota(jnp.int32, (K, LANES), 0).astype(jnp.float32)
    hot = jnp.where(left[K // 2, 1:, :] == index, -1.0, 0.0)
    values = [left[i, :, :] for i in range(K // 2)]
    side = jnp.concatenate([*values, hot], axis=0).T.astype(jnp.bfloat16)
    return side, jnp.broadcast_to(left[K // 2, :1, :], (LANES, LANES)).T


def right_side(right):
    values, lam, ports, columns, weights = of_right(right)
    index = lax.broadcasted_iota(jnp.int32, values.shape, 0).astype(jnp.float32)
    table = jnp.concatenate([jnp.where(ports == index, 1.0, 0.0), values], axis=0).astype(jnp.bfloat16)
    return table, jnp.where(columns == index, weights, 0.0).astype(jnp.bfloat16), lam


def sketch_terms(side, freq, table, omega, lam):
    scale = jnp.concatenate([freq] * (lam.shape[1] // LANES), axis=1) - lam
    loewner = dot(side, table, 1, 0) / scale
    terms = dot(omega, jnp.concatenate(pieces(loewner), axis=0), 1, 1)
    return sum(jnp.split(terms, 3, axis=1)[::-1])


def local_body(*refs):
    lefts, (right, side_out, freq_out, table_out, omega_out, total, cross) = refs[:-7], refs[-7:]
    table, omega, lam = right_side(right)
    table_out[...] = table
    omega_out[...] = omega
    for q, left in enumerate(lefts):
        span = slice(q * LANES, (q + 1) * LANES)
        side, freq = left_side(left)
        side_out[span, :] = side
        freq_out[span, :] = freq
        total[:, span] = sketch_terms(side, freq, table, omega, lam)
    cross[...] = dot(omega, table[K:, :], 1, 1)


def remote_body(*refs):
    side, freq, right, total_in, cross_in, table_out, omega_out, total, cross = refs
    table, omega, lam = right_side(right)
    table_out[...] = table
    omega_out[...] = omega
    for q in range(side.shape[0] // LANES):
        span = slice(q * LANES, (q + 1) * LANES)
        total[:, span] = total_in[:, span] + sketch_terms(side[span, :], freq[span, :], table, omega, lam)
    cross[...] = cross_in[...] + dot(omega, table[K:, :], 1, 1)


def sketch_body(distance, *refs):
    count = (len(refs) - 11) // 2
    owns, gots = refs[:count], refs[count : 2 * count]
    near, far, near_table, near_omega, far_table, far_omega, total, cross, pay, freq_row, port_row = refs[2 * count :]
    table = jnp.concatenate([near_table[...], far_table[...]], axis=1)
    omega = jnp.concatenate([near_omega[...], far_omega[...]], axis=1)
    lam = jnp.concatenate([of_right(near)[1], of_right(far)[1]], axis=1)
    here = lax.rem(lax.div(lax.axis_index("blk"), distance), 2) == 0
    for q in range(count):
        own = total[:, q * LANES : (q + 1) * LANES]
        got = sketch_terms(*left_side(gots[q]), table, omega, lam)
        for place, flip in ((q, False), (count + q, True)):
            spot = slice(place * K, (place + 1) * K)
            pay[spot, :] = jnp.where(here != flip, own, got)
            for out, row in ((freq_row, 0), (port_row, 1)):
                out[place : place + 1, :] = jnp.where(
                    here != flip, owns[q][K // 2, row : row + 1, :], gots[q][K // 2, row : row + 1, :]
                )
    pay[2 * count * K :, :] = jnp.concatenate([cross[: K // 2, :], cross[K // 2 :, :]], axis=1)


def moments_body(own, other, freq, ports, gc, full):
    n_left = freq.shape[0]
    both = own[...] + other[...]
    index = lax.broadcasted_iota(jnp.int32, (K, LANES), 0).astype(jnp.float32)
    cross = both[n_left * K :, :]
    cross = pieces(jnp.concatenate([cross[:, :K], cross[:, K:]], axis=0))
    sketches, shifts = [], []
    for q in range(n_left):
        sketch = both[q * K : (q + 1) * K, :]
        hot = jnp.where(ports[q : q + 1, :] == index, 1.0, 0.0).astype(jnp.bfloat16)
        shift = freq[q : q + 1, :] * sketch
        for piece in cross:
            shift = shift + dot(piece, hot, 1, 0)
        sketches.append(sketch)
        shifts.append(shift)
    sketch = jnp.concatenate(sketches, axis=1)
    h, m, l = pieces(sketch)
    p, q, r = pieces(jnp.concatenate([sketch, jnp.concatenate(shifts, axis=1)], axis=0))
    terms = jnp.split(dot(jnp.concatenate([l, m, h], axis=0), p, 1, 1), 3, axis=0)
    terms += jnp.split(dot(jnp.concatenate([m, h], axis=0), q, 1, 1), 2, axis=0)
    low = (terms[0] + terms[3]) + dot(h, r, 1, 1)
    gc[...] = terms[2] + ((terms[1] + terms[4]) + low)
    full[...] = both[: n_left * K, :]


def full(value):
    return jnp.broadcast_to(value, (SUB, LANES))


def inverse_factor(gram, spread):
    lane = lax.broadcasted_iota(jnp.int32, (SUB, LANES), 1)
    sub = lax.broadcasted_iota(jnp.int32, (SUB, LANES), 0)
    count = K // SUB
    blocks = [
        jnp.where(lane < K, gram[r * SUB : (r + 1) * SUB, :], jnp.where(lane == sub + (K + r * SUB), 1.0, 0.0))
        for r in range(count)
    ]
    out = []
    for r in range(count):
        here, first, base = blocks[r], r * SUB, r * SUB * (SUB + 1)
        below = range(r + 1, count)
        for u in range(SUB):
            spread[base + u * SUB : base + (u + 1) * SUB, :] = full(here[:, first + u : first + u + 1])
        last = base + SUB * SUB
        spread[last : last + SUB, :] = here
        part = {(t, u): full(spread[base + u * SUB + t : base + u * SUB + t + 1, :]) for t in range(SUB) for u in range(t + 1)}
        rows = [full(spread[last + t : last + t + 1, :]) for t in range(SUB)]
        cols = {q: [full(blocks[q][:, first + u : first + u + 1]) for u in range(SUB)] for q in below}
        inverse = []
        for u in range(SUB):
            inverse.append(1.0 / part[u, u])
            ratio = {t: part[t, u] * inverse[u] for t in range(u + 1, SUB)}
            for t in range(u + 1, SUB):
                for v in range(u + 1, t + 1):
                    if t == u + 1:
                        part[t, v] = part[t, v] - (part[t, u] * part[v, u]) * inverse[u]
                    else:
                        part[t, v] = part[t, v] - ratio[t] * part[v, u]
            for t in range(u + 1, SUB):
                rows[t] = rows[t] - ratio[t] * rows[u]
                for q in below:
                    cols[q][t] = cols[q][t] - ratio[t] * cols[q][u]
        done, pivot = rows[0], part[0, 0]
        for t in range(1, SUB):
            done, pivot = jnp.where(sub == t, rows[t], done), jnp.where(sub == t, part[t, t], pivot)
        out.append((done * lax.rsqrt(pivot))[:, K:])
        rows = [row * inv for row, inv in zip(rows, inverse)]
        for q in below:
            terms = [col * row for col, row in zip(cols[q], rows)]
            while len(terms) > 1:
                terms = [a + b for a, b in zip(terms[::2], terms[1::2])]
            blocks[q] = blocks[q] - terms[0]
    return jnp.concatenate(out, axis=0)


def finish_body(scale, own, first, second, third, sketch, basis, projected, spread):
    gc = ((own[...] + first[...]) + (second[...] + third[...])) * scale
    inverse = inverse_factor(gc, spread)
    mine = pl.multiple_of(lax.div(lax.axis_index("blk"), 2) * K, K)
    both = product(inverse, jnp.concatenate([sketch[pl.ds(mine, K), :], gc[:, K:]], axis=1))
    basis[...] = both[:, :LANES]
    projected[...] = product(inverse.T, both[:, LANES:])


def per_device(left_points, left_ports, left_values, right_points, right_ports, right_values, sketch_block, sketch_weight):
    f32 = jnp.float32
    rows, rights = left_points.shape[0], right_points.shape[0]
    blk, wide = lax.axis_size("blk"), lax.axis_size("wide")
    along = (rights // LANES, LANES)
    left, right = kernel_call(
        pack_body,
        (jax.ShapeDtypeStruct((K // 2 + 1, 2, LANES), f32), jax.ShapeDtypeStruct(((K + 4) * along[0], LANES), f32)),
        tuple(pltpu.with_memory_space_constraint(v, pltpu.HBM) for v in (
            left_points.reshape(1, rows),
            left_ports.reshape(1, rows),
            left_values.T,
            right_points.reshape(along),
            right_ports.reshape(along),
            right_values.T,
            sketch_block.reshape(along),
            sketch_weight.reshape(along),
        )),
        in_specs=[pl.BlockSpec(memory_space=pltpu.HBM)] * 8,
        scratch_shapes=[
            pltpu.VMEM((1, rows), f32),
            pltpu.VMEM((1, rows), jnp.int32),
            pltpu.VMEM((K, rows), left_values.dtype),
            pltpu.VMEM(along, f32),
            pltpu.VMEM(along, jnp.int32),
            pltpu.VMEM((K, rights), right_values.dtype),
            pltpu.VMEM(along, jnp.int32),
            pltpu.VMEM(along, sketch_weight.dtype),
            pltpu.SemaphoreType.DMA((8,)),
        ],
    )
    place = lax.axis_index("blk")
    lefts, distance = [left], 2
    while True:
        got = [swap(v, distance) for v in lefts]
        if distance * 2 >= blk:
            break
        here = (place // distance) % 2 == 0
        lefts = [jnp.where(here, a, b) for a, b in zip(lefts, got)] + [jnp.where(here, b, a) for a, b in zip(lefts, got)]
        distance *= 2
    other = swap(right, 1)
    count = len(lefts)
    held = 2 * count
    local = kernel_call(
        local_body,
        (
            jax.ShapeDtypeStruct((count * LANES, LANES), jnp.bfloat16),
            jax.ShapeDtypeStruct((count * LANES, LANES), f32),
            jax.ShapeDtypeStruct((2 * K, rights), jnp.bfloat16),
            jax.ShapeDtypeStruct((K, rights), jnp.bfloat16),
            jax.ShapeDtypeStruct((K, count * LANES), f32),
            jax.ShapeDtypeStruct((K, K), f32),
        ),
        (*lefts, right),
    )
    side, freq, table, omega, total, cross = local
    far_table, far_omega, total, cross = kernel_call(
        remote_body,
        (
            jax.ShapeDtypeStruct(table.shape, table.dtype),
            jax.ShapeDtypeStruct(omega.shape, omega.dtype),
            jax.ShapeDtypeStruct(total.shape, f32),
            jax.ShapeDtypeStruct(cross.shape, f32),
        ),
        (side, freq, other, total, cross),
    )
    pay, freq, ports = kernel_call(
        functools.partial(sketch_body, distance),
        (
            jax.ShapeDtypeStruct((held * K + K // 2, LANES), f32),
            jax.ShapeDtypeStruct((held, LANES), f32),
            jax.ShapeDtypeStruct((held, LANES), f32),
        ),
        (*lefts, *got, right, other, table, omega, far_table, far_omega, total, cross),
    )
    step = 2
    while step < distance:
        pay = pay + swap(pay, step)
        step *= 2
    gc, sketch = kernel_call(
        moments_body,
        (jax.ShapeDtypeStruct((K, LANES), f32), jax.ShapeDtypeStruct((held * K, LANES), f32)),
        (pay, swap(pay, distance), freq, ports),
    )
    gc = gc + swap(gc, 0, 1)
    hops, distance = [(1, 1)], 2
    while distance < wide:
        hops.append((0, distance + 1))
        distance *= 2
    for hop in hops[:-2]:
        gc = gc + swap(gc, *hop)
    (b0, w0), (b1, w1) = hops[-2:]
    parts = [gc]
    for b, w in ((b0, w0), (b1, w1), (b0 ^ b1, w0 ^ w1 ^ 1)):
        parts.append(swap(gc, b, w))
    basis, projected = kernel_call(
        functools.partial(finish_body, 1.0 / (rows * blk * wide)),
        (jax.ShapeDtypeStruct((K, rows), f32), jax.ShapeDtypeStruct((K, K), f32)),
        (*parts, sketch),
        scratch_shapes=[pltpu.VMEM((K * (SUB + 1), LANES), f32)],
    )
    return basis.T, projected


def solution(mesh):
    split = P(("wide", "blk"))
    return jax.shard_map(
        per_device,
        mesh=mesh,
        in_specs=(split, split, P(("wide", "blk"), None), P("blk"), P("blk"), P("blk", None), P("blk"), P("blk")),
        out_specs=(P(("wide", "blk"), None), P()),
        check_vma=False,
    )
```
